512 devices in a mesh: orbit: 8 (over x, core), lon: 64 (over y, z).
Axes of the slice: x: 4, y: 4, z: 16, core: 2. Of those that a mesh axis runs over, the one named last changes fastest.
Arguments:
- interp: bfloat16 [256, 64, 256, 128], P('orbit', 'lon'), may hold values from -0.5 to 0.5
- obs_value: float32 [256, 64, 256], P('orbit', 'lon'), may hold values from -20 to 20
- obs_weight: float32 [256, 64, 256], P('orbit', 'lon'), may hold values from 0.5 to 4
- block_map: int32 [256, 64], P('orbit', 'lon'), may hold values from 0 to 511
- live_count: int32 [8, 64], P('orbit', 'lon'), may hold values from 4 to 32, as said below
- kappa2: float32 [4096, 1024], P('lon'), may hold values from 0.01 to 1
Outputs:
- solution: float32 [4096, 1024], P('lon')
- residual: float32 [4096, 1024], P('lon')
The draws below stay inside these ranges and needn't reach their ends.
Inputs may be any that keep to these rules, and one draw needn't show every extreme that they name: `live_count`: live blocks of the device of orbit group o in band l; its slots at or beyond this count are padding; some device holds exactly 32.
All inputs are finite; a program needn't handle non-finite values.
Results may differ from the reference program's by a relative error of at most 0.014.
Values sent between devices are 32-bit elements; how exact they have to be, the bound alone decides.
A program may use at most 64 MiB of HBM per device.

```python
import math
import jax
import jax.numpy as jnp
from jax import lax

LAT = 1024
OB_DEV = 32
OBS_BLK = 256
CELL_BLK = 128
ITERS = 2
BANDS = 64
ORBITS = 8
NLON = 4096
OBS_BLOCKS = 256
NB_DEV = 512


def draw_obs_value(key, part):
    ramp = 1.0 + 2.0 * jnp.arange(BANDS, dtype=jnp.float32) / max(BANDS - 1, 1)
    base = jnp.clip(jax.random.normal(key, (OBS_BLOCKS, BANDS, OBS_BLK), jnp.float32), -4.0, 4.0)
    return base * ramp[None, :, None]


def draw_live_count(key, part):
    lowest = max(1, OB_DEV // 8)
    first_key, second_key, orbit_key, band_key = jax.random.split(jax.random.fold_in(key, 17), 4)
    first = jax.random.randint(first_key, (ORBITS, BANDS), lowest, OB_DEV + 1)
    second = jax.random.randint(second_key, (ORBITS, BANDS), lowest, OB_DEV + 1)
    counts = jnp.minimum(first, second).astype(jnp.int32)
    orbit_pick = jax.random.randint(orbit_key, (), 0, ORBITS)
    band_pick = jax.random.randint(band_key, (), 0, BANDS)
    return counts.at[orbit_pick, band_pick].set(OB_DEV)


def place_ends(values, key, smallest, largest):
    index_at = [jax.random.randint(jax.random.fold_in(key, axis), (), 0, length) for axis, length in enumerate(values.shape)]
    widest = values.shape.index(max(values.shape))
    neighbour = index_at[:widest] + [(index_at[widest] + 1) % values.shape[widest]] + index_at[widest + 1:]
    return values.at[tuple(index_at)].set(smallest).at[tuple(neighbour)].set(largest)


def steps_of(key, extent, pieces, least, largest):
    gain = 1.0
    for position, blocks in pieces:
        steps = jax.random.uniform(jax.random.fold_in(jax.random.fold_in(key, 6), position), (blocks,), jnp.float32, least / len(pieces), largest / len(pieces))
        gain = gain * jnp.repeat(jnp.exp(steps), extent[position] // blocks).reshape((-1,) + (1,) * (len(extent) - 1 - position))
    return gain


def noise(stream_key, dims, width, limit, pieces=(), held_as=jnp.bfloat16):
    values = jax.random.normal(stream_key, dims, jnp.float32) * width
    if len(pieces) > 0:
        values = steps_of(stream_key, dims, pieces, -0.22, 0.18) * values
    return jnp.clip(values, min=-limit, max=limit).astype(held_as)


def setup_inputs(seed: int = 0) -> dict:
    key_list = jax.random.split(jax.random.key(seed), 7)
    interp = noise(key_list[0], (OBS_BLOCKS, BANDS, OBS_BLK, CELL_BLK), CELL_BLK ** -0.5, 0.5, ((0, 8), (1, 64)))
    obs_value = draw_obs_value(jax.random.fold_in(key_list[6], 71), 0)
    obs_weight = jnp.clip(jnp.exp(math.log(4.0) - 2.0794415 * jax.random.uniform(key_list[2], (OBS_BLOCKS, BANDS, OBS_BLK), jnp.float32) ** steps_of(key_list[2], (OBS_BLOCKS, BANDS, OBS_BLK), ((0, 8), (1, 64)), -0.2, 0.2)), 0.5, 4.0)
    block_map = place_ends(jax.random.randint(key_list[3], (OBS_BLOCKS, BANDS), 0, NB_DEV), jax.random.fold_in(key_list[3], 1), 0, NB_DEV - 1).astype(jnp.int32)
    live_count = draw_live_count(jax.random.fold_in(key_list[6], 71), 0)
    kappa2 = jnp.clip(jnp.exp(math.log(1.0) - 4.6051702 * jax.random.uniform(key_list[5], (NLON, LAT), jnp.float32) ** steps_of(key_list[5], (NLON, LAT), ((0, 64),), -0.2, 0.2)), 0.01, 1.0)
    return dict(interp=interp, obs_value=obs_value, obs_weight=obs_weight, block_map=block_map, live_count=live_count, kappa2=kappa2)


prior_weight = 0.0625


def stencil(field, kappa2):
    padded = jnp.pad(field, ((0, 0), (1, 1)))
    lat_pair = padded[:, 2:] + padded[:, :-2]
    return (kappa2 + 4.0) * field - jnp.roll(field, 1, 0) - jnp.roll(field, -1, 0) - lat_pair


def prior_term(field, kappa2):
    return prior_weight * stencil(stencil(field, kappa2), kappa2)


def live_mask(live_count):
    slot_index = jnp.arange(OBS_BLOCKS) % OB_DEV
    group_index = jnp.arange(OBS_BLOCKS) // OB_DEV
    return (slot_index[:, None] < live_count[group_index, :]).astype(jnp.float32)


def take_band(array, band):
    return lax.dynamic_index_in_dim(array, band, 1, keepdims=False)


def data_terms(interp, obs_value, obs_weight, block_map, live):
    scaled = lax.optimization_barrier((obs_weight * obs_value).astype(jnp.bfloat16)).astype(jnp.float32)

    def per_band(band):
        matrices = take_band(interp, band).astype(jnp.float32)
        weights = take_band(obs_weight, band)
        targets = take_band(block_map, band)
        active = take_band(live, band)
        first = jnp.einsum('sqc,sq->sc', matrices, take_band(scaled, band), precision=lax.Precision.HIGHEST) * active[:, None]
        second = jnp.einsum('sqc,sq->sc', matrices * matrices, weights, precision=lax.Precision.HIGHEST) * active[:, None]
        zeros = jnp.zeros((NB_DEV, CELL_BLK), jnp.float32)
        return zeros.at[targets].add(first), zeros.at[targets].add(second)

    right_side, obs_diag = lax.map(per_band, jnp.arange(BANDS))
    return right_side.reshape(NLON, LAT), obs_diag.reshape(NLON, LAT)


def normal_term(field, interp, obs_weight, block_map, live):
    rounded = lax.optimization_barrier(field.astype(jnp.bfloat16)).astype(jnp.float32)
    cell_rows = rounded.reshape(BANDS, NB_DEV, CELL_BLK)

    def per_band(band):
        matrices = take_band(interp, band).astype(jnp.float32)
        weights = take_band(obs_weight, band)
        targets = take_band(block_map, band)
        active = take_band(live, band)
        band_cells = lax.dynamic_index_in_dim(cell_rows, band, 0, keepdims=False)
        picked = band_cells[targets]
        predicted = jnp.einsum('sqc,sc->sq', matrices, picked, precision=lax.Precision.HIGHEST)
        scaled = lax.optimization_barrier((weights * predicted).astype(jnp.bfloat16)).astype(jnp.float32)
        back = jnp.einsum('sqc,sq->sc', matrices, scaled, precision=lax.Precision.HIGHEST) * active[:, None]
        return jnp.zeros((NB_DEV, CELL_BLK), jnp.float32).at[targets].add(back)

    return lax.map(per_band, jnp.arange(BANDS)).reshape(NLON, LAT)


def reference(interp, obs_value, obs_weight, block_map, live_count, kappa2):
    live = live_mask(live_count)
    right_side, obs_diag = data_terms(interp, obs_value, obs_weight, block_map, live)
    precond = prior_weight * ((kappa2 + 4.0) ** 2 + 4.0) + obs_diag

    def system(field):
        return prior_term(field, kappa2) + normal_term(field, interp, obs_weight, block_map, live)

    solution = jnp.zeros_like(right_side)
    residual = right_side
    scaled_res = residual / precond
    direction = scaled_res
    product_now = jnp.sum(residual * scaled_res)
    for turn in range(ITERS):
        image = system(direction)
        alpha = product_now / jnp.sum(direction * image)
        solution = solution + alpha * direction
        residual = residual - alpha * image
        if turn + 1 < ITERS:
            scaled_res = residual / precond
            product_next = jnp.sum(residual * scaled_res)
            direction = scaled_res + (product_next / product_now) * direction
            product_now = product_next
    return solution, residual
```

```python
import functools

import jax
import jax.numpy as jnp
from jax import lax
from jax.experimental import pallas as pl
from jax.experimental.pallas import tpu as pltpu
from jax.sharding import PartitionSpec as P

MESH = pl.DeviceIdType.MESH
F32 = jnp.float32
BF16 = jnp.bfloat16

prior_weight = 0.0625
SUB = 8
CHUNKS = 4


def split(value):
    high = value.astype(BF16)
    return high, (value - high.astype(F32)).astype(BF16)


def lat_pair(cells, lane, sub):
    up = pltpu.roll(cells, 127, axis=2)
    down = pltpu.roll(cells, 1, axis=2)
    up_edge = jnp.where(sub == SUB - 1, 0.0, pltpu.roll(up, SUB - 1, axis=1))
    down_edge = jnp.where(sub == 0, 0.0, pltpu.roll(down, 1, axis=1))
    return jnp.where(lane == 127, up_edge, up) + jnp.where(lane == 0, down_edge, down)


def stencil(source, source_row, kappa, kappa_row, rows):
    shape = (rows, SUB, 128)
    lane = lax.broadcasted_iota(jnp.int32, shape, 2)
    sub = lax.broadcasted_iota(jnp.int32, shape, 1)

    def part(ref, row):
        return ref[pl.ds(pl.multiple_of(row * SUB, SUB), rows * SUB), :].reshape(shape)

    center = part(source, source_row)
    around = part(source, source_row + 1) + part(source, source_row - 1)
    return (part(kappa, kappa_row) + 4.0) * center - around - lat_pair(center, lane, sub)


def kernel(
    dims, interp, value, weight, targets, count, kappa, out_solution, out_residual,
    blocks, values, weights, kappa_in, kap, grams, hot,
    codes, gather_one, gather_two, gather_three,
    right, inverse, z_own, z_ext, k_ext, y_own, w_own, w_ext, q_own,
    picks, sums, wide, plane_stats, column_stats,
    load_sem, orbit_send, orbit_recv, halo_send, halo_recv,
    plane_send, plane_recv, column_send, column_recv,
):
    orbits, ys, zs = dims
    slots = weights.shape[0]
    obs = weights.shape[2]
    rows = kappa_in.shape[0]
    tiles = rows * SUB
    plane = orbits * ys
    lons = ys * zs
    orbit = lax.axis_index("orbit")
    lon = lax.axis_index("lon")
    y = lon // zs
    z = lax.rem(lon, zs)
    east = lax.rem(lon + 1, lons)
    west = lax.rem(lon + lons - 1, lons)
    me_plane = orbit * ys + y

    per_chunk = slots // CHUNKS
    load_w = pltpu.make_async_copy(weight, weights, load_sem.at[0])
    load_v = pltpu.make_async_copy(value, values, load_sem.at[1])
    load_k = pltpu.make_async_copy(kappa, kappa_in, load_sem.at[2])
    load_w.start()
    load_v.start()
    loads = []
    for chunk in range(CHUNKS):
        part = pl.ds(chunk * per_chunk, per_chunk)
        loads.append(pltpu.make_async_copy(interp.at[part], blocks.at[part], load_sem.at[3 + chunk]))
        loads[-1].start()
    load_k.start()

    barrier = pltpu.get_barrier_semaphore()

    def plane_peer(step):
        there = lax.rem(me_plane + step, plane)
        return (there // ys, lax.rem(there, ys) * zs + z)

    def column_peer(step):
        return (orbit, y * zs + lax.rem(z + step, zs))

    @pl.loop(1, plane)
    def _(step):
        pl.semaphore_signal(barrier, inc=1, device_id=plane_peer(step), device_id_type=MESH)

    @pl.loop(1, zs)
    def _(step):
        pl.semaphore_signal(barrier, inc=1, device_id=column_peer(step), device_id_type=MESH)

    for side in (east, west):
        pl.semaphore_signal(barrier, inc=1, device_id=(orbit, side), device_id_type=MESH)

    lane_row = lax.broadcasted_iota(jnp.int32, (1, 128), 1)
    first_lane = lax.rem(orbit, 128 // slots) * slots
    live = count[0]
    code = jnp.zeros((1, 128), jnp.int32)
    for slot in range(slots):
        code = jnp.where(lane_row == first_lane + slot, targets[slot] + 1, code)
    code = jnp.where(lane_row - first_lane < live, code, 0)
    codes[orbit] = code.astype(F32)

    load_w.wait()
    load_v.wait()
    eye = lax.broadcasted_iota(jnp.int32, (128, 128), 0) == lax.broadcasted_iota(jnp.int32, (128, 128), 1)
    for chunk in range(CHUNKS):
        loads[chunk].wait()

        @pl.loop(chunk * per_chunk, (chunk + 1) * per_chunk)
        def _(slot):
            block = blocks[slot]
            weight_row = weights[slot]
            data = (weight_row * values[slot]).astype(BF16)
            high, low = split(block.T.astype(F32) * weight_row)
            left = jnp.concatenate([high, low, jnp.broadcast_to(data, (16, obs))], axis=0)
            product = jnp.dot(left, block, preferred_element_type=F32)
            factor = jnp.where(slot < live, 1.0, 0.0)
            gram = (product[:128] + product[128:256]) * factor
            grams[slot] = gram
            gather_one[orbit, pl.ds(slot, 1), :] = product[256:257] * factor
            gather_one[orbit, pl.ds(slots + slot, 1), :] = jnp.sum(
                jnp.where(eye, gram, 0.0), axis=0, keepdims=True
            )

    load_k.wait()

    @pl.loop(0, rows // SUB)
    def _(group):
        for tile in range(SUB):
            kap[pl.ds((group * SUB + 1) * SUB + tile, SUB, stride=SUB), :] = kappa_in[
                pl.ds(pl.multiple_of(group * SUB, SUB), SUB), tile * 128 : (tile + 1) * 128
            ]

    pl.semaphore_wait(barrier, (plane - 1) + (zs - 1) + 2)

    def orbit_copy(buffer, which, step):
        return pltpu.make_async_remote_copy(
            src_ref=buffer.at[orbit],
            dst_ref=buffer.at[orbit],
            send_sem=orbit_send.at[which, step],
            recv_sem=orbit_recv.at[which, step],
            device_id=(lax.rem(orbit + step, orbits), lon),
            device_id_type=MESH,
        )

    def orbit_start(buffer, which):
        for step in range(1, orbits):
            orbit_copy(buffer, which, step).start()

    def orbit_wait(buffer, which):
        for step in range(1, orbits):
            orbit_copy(buffer, which, step).wait_recv()

    def halo_copy(source, source_row, target, target_row, count_rows, which, side, device):
        return pltpu.make_async_remote_copy(
            src_ref=source.at[pl.ds(source_row * SUB, count_rows * SUB)],
            dst_ref=target.at[pl.ds(target_row * SUB, count_rows * SUB)],
            send_sem=halo_send.at[which, side],
            recv_sem=halo_recv.at[which, side],
            device_id=(orbit, device),
            device_id_type=MESH,
        )

    orbit_start(codes, 0)
    orbit_start(gather_one, 1)
    kap_halo = [
        halo_copy(kap, rows, kap, 0, 1, 0, 0, east),
        halo_copy(kap, 1, kap, rows + 1, 1, 0, 1, west),
    ]
    for copy in kap_halo:
        copy.start()

    orbit_wait(codes, 0)
    groups = hot.shape[1] // 128
    per_group = orbits // groups
    for group in range(groups):
        row = codes[group * per_group]
        for member in range(1, per_group):
            row = row + codes[group * per_group + member]
        part = 64

        @pl.loop(0, tiles // part)
        def _(step):
            offset = pl.multiple_of(step * part, part)
            cell = lax.broadcasted_iota(jnp.int32, (part, 128), 0) + (offset + 1)
            hot[pl.ds(offset, part), group * 128 : (group + 1) * 128] = jnp.where(
                cell.astype(F32) == row, 1.0, 0.0
            ).astype(BF16)

    def scatter(terms):
        high, low = split(terms)
        wide[...] = jnp.dot(hot[...], jnp.concatenate([high, low], axis=1), preferred_element_type=F32)

    def slot_rows(buffer, first):
        return buffer[:, first : first + slots, :].reshape(orbits * slots, 128)

    piece = 8 * SUB

    def each_piece(body):
        @pl.loop(0, tiles // piece)
        def _(step):
            body(pl.multiple_of(step * piece, piece))

    def added(offset):
        both = wide[pl.ds(offset, piece), :]
        return both[:, :128] + both[:, 128:]

    orbit_wait(gather_one, 1)
    scatter(slot_rows(gather_one, slots))

    def make_inverse(offset):
        shifted = kap[pl.ds(offset + SUB, piece), :] + 4.0
        inverse[pl.ds(offset, piece), :] = 1.0 / (prior_weight * (shifted * shifted + 4.0) + added(offset))

    each_piece(make_inverse)
    scatter(slot_rows(gather_one, 0))

    def make_z(offset):
        data = added(offset)
        right[pl.ds(offset, piece), :] = data
        scaled = data * inverse[pl.ds(offset, piece), :]
        z_own[pl.ds(offset, piece), :] = scaled
        z_ext[pl.ds(offset + 2 * SUB, piece), :] = scaled

    each_piece(make_z)

    def field_halo(own, ext, which):
        return [
            halo_copy(own, rows - 2, ext, 0, 2, which, 0, east),
            halo_copy(own, 0, ext, rows + 2, 2, which, 1, west),
        ]

    z_halo = field_halo(z_own, z_ext, 1)
    for copy in z_halo:
        copy.start()

    def apply_grams(own, gather):
        for slot in range(slots):
            picks[slot : slot + 1, :] = own[pl.ds(targets[slot], 1), :]
        columns = picks[...].T
        for slot in range(slots):
            column = jnp.broadcast_to(columns[:, slot : slot + 1], (128, 128))
            sums[slot * SUB : (slot + 1) * SUB, :] = jnp.sum(
                (grams[slot] * column).reshape(128 // SUB, SUB, 128), axis=0
            )
        total = sums[pl.ds(0, slots, stride=SUB), :]
        for part in range(1, SUB):
            total = total + sums[pl.ds(part, slots, stride=SUB), :]
        gather[orbit] = total
        return total

    apply_grams(z_own, gather_two)
    orbit_start(gather_two, 2)

    for copy in kap_halo:
        copy.wait_recv()
    for copy in z_halo:
        copy.wait_recv()

    first_rows = 6

    def first_stencil(ext):
        @pl.loop(0, (rows + 2) // first_rows)
        def _(step):
            row = step * first_rows
            k_ext[pl.ds(pl.multiple_of(row * SUB, SUB), first_rows * SUB), :] = stencil(
                ext, row + 1, kap, row, first_rows
            ).reshape(first_rows * SUB, 128)

    def second_stencil(target):
        @pl.loop(0, rows // SUB)
        def _(step):
            row = step * SUB
            target[pl.ds(pl.multiple_of(row * SUB, SUB), SUB * SUB), :] = prior_weight * stencil(
                k_ext, row + 1, kap, row + 1, SUB
            ).reshape(SUB * SUB, 128)

    first_stencil(z_ext)
    second_stencil(y_own)

    orbit_wait(gather_two, 2)
    scatter(slot_rows(gather_two, 0))

    def make_w(offset):
        part = pl.ds(offset, piece)
        image = y_own[part, :] + added(offset)
        y_own[part, :] = image
        scaled = image * inverse[part, :]
        w_own[part, :] = scaled
        w_ext[pl.ds(offset + 2 * SUB, piece), :] = scaled

    each_piece(make_w)
    w_halo = field_halo(w_own, w_ext, 2)
    for copy in w_halo:
        copy.start()

    terms = apply_grams(w_own, gather_three)
    orbit_start(gather_three, 3)
    last = jnp.sum((picks[...][:slots] * terms).reshape(slots // SUB, SUB, 128), axis=0)

    share_rows = rows // orbits
    share_row = orbit * share_rows
    share = pl.ds(pl.multiple_of(share_row * SUB, SUB), share_rows * SUB)

    def folded(product):
        return jnp.sum(product.reshape(share_rows, SUB, 128), axis=0)

    products = [
        folded(right[share, :] * z_own[share, :]),
        folded(y_own[share, :] * z_own[share, :]),
        folded(y_own[share, :] * w_own[share, :]),
    ]
    for copy in w_halo:
        copy.wait_recv()
    own_k = stencil(w_ext, share_row + 2, kap, share_row + 1, share_rows)
    products.append(last + prior_weight * jnp.sum(own_k * own_k, axis=0))
    row_index = lax.broadcasted_iota(jnp.int32, (SUB, 128), 0)
    lane_index = lax.broadcasted_iota(jnp.int32, (SUB, 128), 1)
    stacked = jnp.zeros((SUB, 128), F32)
    for index, product in enumerate(products):
        stacked = jnp.where(row_index == index, jnp.sum(product, axis=0, keepdims=True), stacked)
    stacked = stacked + pltpu.roll(stacked, 64, axis=1)
    stacked = stacked + pltpu.roll(stacked, 32, axis=1)
    packed = jnp.sum(jnp.where(lane_index // 32 == row_index, stacked, 0.0), axis=0, keepdims=True)
    plane_stats[me_plane] = packed

    def plane_copy(step):
        return pltpu.make_async_remote_copy(
            src_ref=plane_stats.at[me_plane],
            dst_ref=plane_stats.at[me_plane],
            send_sem=plane_send.at[step],
            recv_sem=plane_recv.at[step],
            device_id=plane_peer(step),
            device_id_type=MESH,
        )

    def column_copy(step):
        return pltpu.make_async_remote_copy(
            src_ref=column_stats.at[z],
            dst_ref=column_stats.at[z],
            send_sem=column_send.at[step],
            recv_sem=column_recv.at[step],
            device_id=column_peer(step),
            device_id_type=MESH,
        )

    @pl.loop(1, plane)
    def _(step):
        plane_copy(step).start()

    first_stencil(w_ext)

    @pl.loop(1, plane)
    def _(step):
        plane_copy(step).wait_recv()

    total = plane_stats[0]
    for index in range(1, plane):
        total = total + plane_stats[index]
    column_stats[z] = total

    @pl.loop(1, zs)
    def _(step):
        column_copy(step).start()

    second_stencil(q_own)
    orbit_wait(gather_three, 3)
    scatter(slot_rows(gather_three, 0))

    def make_q(offset):
        part = pl.ds(offset, piece)
        q_own[part, :] = q_own[part, :] + added(offset)

    each_piece(make_q)

    @pl.loop(1, zs)
    def _(step):
        column_copy(step).wait_recv()

    total = column_stats[0]
    for index in range(1, zs):
        total = total + column_stats[index]
    g = [
        jnp.sum(jnp.where(lane_row // 32 == index, total, 0.0), axis=1, keepdims=True)
        for index in range(4)
    ]
    alpha = g[0] / g[1]
    later = alpha * alpha * g[2] - g[0]
    grow = 1.0 + later / g[0]
    alpha_later = later / (grow * grow * g[1] - 2.0 * grow * alpha * g[2] + alpha * alpha * g[3])
    on_first = alpha + alpha_later * grow
    on_second = alpha_later * alpha

    def finish(offset):
        part = pl.ds(offset, piece)
        w_own[part, :] = on_first * z_own[part, :] - on_second * w_own[part, :]
        q_own[part, :] = right[part, :] - on_first * y_own[part, :] + on_second * q_own[part, :]

    for copy in w_halo:
        copy.wait_send()
    each_piece(finish)

    @pl.loop(0, rows // SUB)
    def _(group):
        for tile in range(SUB):
            strided = pl.ds(group * SUB * SUB + tile, SUB, stride=SUB)
            place = pl.ds(pl.multiple_of(group * SUB, SUB), SUB)
            out_solution[place, tile * 128 : (tile + 1) * 128] = w_own[strided, :]
            out_residual[place, tile * 128 : (tile + 1) * 128] = q_own[strided, :]

    for which, buffer in enumerate((codes, gather_one, gather_two, gather_three)):
        for step in range(1, orbits):
            orbit_copy(buffer, which, step).wait_send()
    for copy in kap_halo + z_halo:
        copy.wait_send()

    @pl.loop(1, plane)
    def _(step):
        plane_copy(step).wait_send()

    @pl.loop(1, zs)
    def _(step):
        column_copy(step).wait_send()


def solution(mesh):
    return build(mesh, 4, 16)


def build(mesh, ys, zs):
    orbits = mesh.shape["orbit"]

    def per_device(interp, obs_value, obs_weight, block_map, live_count, kappa2):
        slots, _, obs, cells = interp.shape
        rows, lat = kappa2.shape
        tiles = rows * lat // cells
        plane = orbits * ys
        hot_width = max(orbits * slots, 128)
        vmem = pltpu.VMEM
        field = vmem((tiles, 128), F32)
        extended = vmem((tiles + 4 * SUB, 128), F32)
        inner = vmem((tiles + 2 * SUB, 128), F32)
        gather = vmem((orbits, slots, 128), F32)
        return pl.pallas_call(
            functools.partial(kernel, (orbits, ys, zs)),
            out_shape=(
                jax.ShapeDtypeStruct(kappa2.shape, F32),
                jax.ShapeDtypeStruct(kappa2.shape, F32),
            ),
            in_specs=[
                pl.BlockSpec(memory_space=pl.ANY),
                pl.BlockSpec(memory_space=pl.ANY),
                pl.BlockSpec(memory_space=pl.ANY),
                pl.BlockSpec(memory_space=pltpu.SMEM),
                pl.BlockSpec(memory_space=pltpu.SMEM),
                pl.BlockSpec(memory_space=pl.ANY),
            ],
            out_specs=(pl.BlockSpec(memory_space=vmem), pl.BlockSpec(memory_space=vmem)),
            scratch_shapes=[
                vmem((slots, obs, cells), BF16),
                vmem((slots, 1, obs), F32),
                vmem((slots, 1, obs), F32),
                vmem((rows, lat), F32),
                inner,
                vmem((slots, 128, 128), F32),
                vmem((tiles, hot_width), BF16),
                vmem((orbits, 1, 128), F32),
                vmem((orbits, 2 * slots, 128), F32),
                gather,
                gather,
                field,
                field,
                field,
                extended,
                inner,
                field,
                field,
                extended,
                field,
                vmem((slots, 128), F32),
                vmem((slots * SUB, 128), F32),
                vmem((tiles, 256), F32),
                vmem((plane, 1, 128), F32),
                vmem((zs, 1, 128), F32),
                pltpu.SemaphoreType.DMA((3 + CHUNKS,)),
                pltpu.SemaphoreType.DMA((4, orbits)),
                pltpu.SemaphoreType.DMA((4, orbits)),
                pltpu.SemaphoreType.DMA((3, 2)),
                pltpu.SemaphoreType.DMA((3, 2)),
                pltpu.SemaphoreType.DMA((plane,)),
                pltpu.SemaphoreType.DMA((plane,)),
                pltpu.SemaphoreType.DMA((zs,)),
                pltpu.SemaphoreType.DMA((zs,)),
            ],
            compiler_params=pltpu.CompilerParams(
                collective_id=0, has_side_effects=True, vmem_limit_bytes=48 * 1024 * 1024
            ),
        )(
            interp.reshape(slots, obs, cells),
            obs_value,
            obs_weight,
            block_map.reshape(slots),
            live_count.reshape(1),
            kappa2,
        )

    in_specs = (
        P("orbit", "lon", None, None),
        P("orbit", "lon", None),
        P("orbit", "lon", None),
        P("orbit", "lon"),
        P("orbit", "lon"),
        P("lon", None),
    )
    out_specs = (P("lon", None), P("lon", None))
    return jax.shard_map(
        per_device, mesh=mesh, in_specs=in_specs, out_specs=out_specs, check_vma=False
    )
```

```python
import functools

import jax
import jax.numpy as jnp
from jax import lax
from jax.experimental import pallas as pl
from jax.experimental.pallas import tpu as pltpu
from jax.sharding import PartitionSpec as P

MESH = pl.DeviceIdType.MESH
F32 = jnp.float32
BF16 = jnp.bfloat16

prior_weight = 0.0625
SUB = 8
CHUNKS = 4
SPLIT = (12, 24)
SPLIT_OF = 32


def split(value):
    high = value.astype(BF16)
    return high, (value - high.astype(F32)).astype(BF16)


def lat_pair(cells, lane, sub):
    up = pltpu.roll(cells, 127, axis=2)
    down = pltpu.roll(cells, 1, axis=2)
    up_edge = jnp.where(sub == SUB - 1, 0.0, pltpu.roll(up, SUB - 1, axis=1))
    down_edge = jnp.where(sub == 0, 0.0, pltpu.roll(down, 1, axis=1))
    return jnp.where(lane == 127, up_edge, up) + jnp.where(lane == 0, down_edge, down)


def stencil(source, source_row, kappa, kappa_row, rows):
    shape = (rows, SUB, 128)
    lane = lax.broadcasted_iota(jnp.int32, shape, 2)
    sub = lax.broadcasted_iota(jnp.int32, shape, 1)

    def part(ref, row):
        return ref[pl.ds(pl.multiple_of(row * SUB, SUB), rows * SUB), :].reshape(shape)

    center = part(source, source_row)
    around = part(source, source_row + 1) + part(source, source_row - 1)
    return (part(kappa, kappa_row) + 4.0) * center - around - lat_pair(center, lane, sub)


def kernel(
    dims, interp, value, weight, targets_hbm, count_hbm, kappa, out_solution, out_residual,
    targets, count, blocks, values, weights, kappa_in, kap_own, kap, grams, hot, match,
    codes, gather_one, gather_two, gather_three,
    right, inverse, z_own, z_ext, k_ext, y_own, w_own, w_edge, w_ext, q_own,
    kap_picks, inverse_picks, picks, sums, wide, plane_stats, column_stats,
    load_sem, orbit_send, orbit_recv, one_send, one_recv, halo_send, halo_recv,
    plane_send, plane_recv, column_send, column_recv, known,
):
    orbits, ys, zs = dims
    xs = orbits // 2
    slots = weights.shape[0]
    obs = weights.shape[2]
    rows = kappa_in.shape[0]
    tiles = rows * SUB
    plane = orbits * ys
    lons = ys * zs
    orbit = lax.axis_index("orbit")
    lon = lax.axis_index("lon")
    x = orbit // 2
    core = lax.rem(orbit, 2)
    y = lon // zs
    z = lax.rem(lon, zs)
    east = lax.rem(lon + 1, lons)
    west = lax.rem(lon + lons - 1, lons)
    me_plane = orbit * ys + y

    per_chunk = slots // CHUNKS
    load_t = pltpu.make_async_copy(targets_hbm, targets, load_sem.at[3 + CHUNKS])
    load_c = pltpu.make_async_copy(count_hbm, count, load_sem.at[4 + CHUNKS])
    load_w = pltpu.make_async_copy(weight, weights, load_sem.at[0])
    load_v = pltpu.make_async_copy(value, values, load_sem.at[1])
    load_k = pltpu.make_async_copy(kappa, kappa_in, load_sem.at[2])
    load_w.start()
    load_v.start()
    loads = []
    for chunk in range(CHUNKS):
        part = pl.ds(chunk * per_chunk, per_chunk)
        loads.append(pltpu.make_async_copy(interp.at[part], blocks.at[part], load_sem.at[3 + chunk]))
        loads[-1].start()
    load_t.start()
    load_c.start()
    load_k.start()

    def plane_peer(step):
        there = lax.rem(me_plane + step, plane)
        return (there // ys, lax.rem(there, ys) * zs + z)

    def column_peer(step):
        return (orbit, y * zs + lax.rem(z + step, zs))

    def signal(semaphore, device):
        pl.semaphore_signal(semaphore, inc=1, device_id=device, device_id_type=MESH)

    def both_ways(step):
        return sorted({step % zs, -step % zs} - {0})

    def learned(which, step):
        if both_ways(step):
            pl.semaphore_wait(known.at[which], len(both_ways(step)))

    barrier = pltpu.get_barrier_semaphore()
    near = [(lax.rem(orbit + step, orbits), lon) for step in range(1, orbits)]
    near += [(orbit, lax.rem(y + step, ys) * zs + z) for step in range(1, ys)]
    near += [column_peer(step) for step in sorted({1 % zs, -1 % zs, 2 % zs, -2 % zs} - {0})]
    near += [(orbit, east), (orbit, west)]
    for device in near:
        signal(barrier, device)

    load_w.wait()
    load_v.wait()
    load_c.wait()
    live = count[0, 0]
    first_row = lax.broadcasted_iota(jnp.int32, (16, obs), 0) == 0
    for chunk in range(CHUNKS):
        loads[chunk].wait()

        @pl.loop(chunk * per_chunk, (chunk + 1) * per_chunk, unroll=2)
        def _(slot):
            block = blocks[slot]
            weight_row = weights[slot]
            left = jnp.where(first_row, weight_row * values[slot], weight_row).astype(BF16)
            product = jnp.dot(
                left, jnp.concatenate([block, block * block], axis=1), preferred_element_type=F32
            )
            factor = jnp.where(slot < live, 1.0, 0.0)
            gather_one[orbit, pl.ds(slot, 1), :] = product[0:1, :128] * factor
            gather_one[orbit, pl.ds(slots + slot, 1), :] = product[1:2, 128:] * factor

    load_t.wait()
    lane_row = lax.broadcasted_iota(jnp.int32, (1, 128), 1)
    first_lane = lax.rem(orbit, 128 // slots) * slots
    code = jnp.zeros((1, 128), jnp.int32)
    for slot in range(slots):
        code = jnp.where(lane_row == first_lane + slot, targets[slot] + 1, code)
    code = jnp.where(lane_row - first_lane < live, code, 0)
    codes[orbit] = code.astype(F32)

    pl.semaphore_wait(barrier, len(near))

    def orbit_copy(buffer, which, step):
        return pltpu.make_async_remote_copy(
            src_ref=buffer.at[orbit],
            dst_ref=buffer.at[orbit],
            send_sem=orbit_send.at[which, step],
            recv_sem=orbit_recv.at[which, step],
            device_id=(lax.rem(orbit + step, orbits), lon),
            device_id_type=MESH,
        )

    def orbit_start(buffer, which):
        for step in range(1, orbits):
            orbit_copy(buffer, which, step).start()

    def orbit_wait(buffer, which):
        for step in range(1, orbits):
            orbit_copy(buffer, which, step).wait_recv()

    def one_copy(owner, device, index):
        return pltpu.make_async_remote_copy(
            src_ref=gather_one.at[owner],
            dst_ref=gather_one.at[owner],
            send_sem=one_send.at[index],
            recv_sem=one_recv.at[index],
            device_id=(device, lon),
            device_id_type=MESH,
        )

    def along(step):
        return lax.rem(x + step + xs, xs) * 2 + core

    partner = x * 2 + 1 - core
    x_steps = sorted(range(1, xs), key=lambda step: min(step, xs - step))
    own_copies = [one_copy(orbit, along(step), step) for step in reversed(x_steps)]
    own_copies.append(one_copy(orbit, partner, 0))
    for copy in own_copies:
        copy.start()
    orbit_start(codes, 0)
    for step in both_ways(2):
        signal(known.at[0], column_peer(step))

    def halo_copy(source, source_row, target, target_row, count_rows, which, side, device):
        return pltpu.make_async_remote_copy(
            src_ref=source.at[pl.ds(source_row * SUB, count_rows * SUB)],
            dst_ref=target.at[pl.ds(target_row * SUB, count_rows * SUB)],
            send_sem=halo_send.at[which, side],
            recv_sem=halo_recv.at[which, side],
            device_id=(orbit, device),
            device_id_type=MESH,
        )

    load_k.wait()

    @pl.loop(0, rows // SUB)
    def _(group):
        for tile in range(SUB):
            values_here = kappa_in[
                pl.ds(pl.multiple_of(group * SUB, SUB), SUB), tile * 128 : (tile + 1) * 128
            ]
            kap[pl.ds((group * SUB + 1) * SUB + tile, SUB, stride=SUB), :] = values_here
            kap_own[pl.ds(group * SUB * SUB + tile, SUB, stride=SUB), :] = values_here

    kap_halo = [
        halo_copy(kap_own, rows - 1, kap, 0, 1, 0, 0, east),
        halo_copy(kap_own, 0, kap, rows + 1, 1, 0, 1, west),
    ]
    for copy in kap_halo:
        copy.start()

    def pick(own, target):
        for slot in range(slots):
            target[slot : slot + 1, :] = own[pl.ds(targets[slot], 1), :]

    pick(kap_own, kap_picks)

    def make_grams(begin, end):
        @pl.loop(begin, end)
        def _(slot):
            block = blocks[slot]
            high, low = split(block.T.astype(F32) * weights[slot])
            product = jnp.dot(jnp.concatenate([high, low], axis=0), block, preferred_element_type=F32)
            grams[slot] = (product[:128] + product[128:]) * jnp.where(slot < live, 1.0, 0.0)

    forwards = []

    def forward(step):
        one_copy(orbit, along(step), step).wait_recv()
        forwards.append(one_copy(along(-step), partner, xs - 1 + step))
        forwards[-1].start()

    cuts = [0] + [slots * part // SPLIT_OF for part in SPLIT] + [slots]
    make_grams(cuts[0], cuts[1])

    orbit_wait(codes, 0)
    groups = hot.shape[1] // 128
    per_group = orbits // groups
    for group in range(groups):
        row = codes[group * per_group]
        for member in range(1, per_group):
            row = row + codes[group * per_group + member]
        part = 64
        columns = slice(group * 128, (group + 1) * 128)
        for slot in range(slots):
            wanted = (targets[slot] + 1).astype(F32)
            match[slot : slot + 1, columns] = jnp.where(row == wanted, 1.0, 0.0)

        @pl.loop(0, tiles // part)
        def _(step):
            offset = pl.multiple_of(step * part, part)
            cell = lax.broadcasted_iota(jnp.int32, (part, 128), 0) + (offset + 1)
            hot[pl.ds(offset, part), columns] = jnp.where(cell.astype(F32) == row, 1.0, 0.0).astype(BF16)

    for step in x_steps[:2]:
        forward(step)
    make_grams(cuts[1], cuts[2])
    for step in x_steps[2:]:
        forward(step)
    make_grams(cuts[2], cuts[3])

    def halves(terms):
        return jnp.concatenate(split(terms), axis=1)

    def joined(product):
        return product[:, :128] + product[:, 128:]

    def scatter(terms):
        wide[...] = jnp.dot(hot[...], halves(terms), preferred_element_type=F32)

    def slot_rows(buffer, first):
        return buffer[:, first : first + slots, :].reshape(orbits * slots, 128)

    piece = 8 * SUB

    def each_piece(body):
        @pl.loop(0, tiles // piece)
        def _(step):
            body(pl.multiple_of(step * piece, piece))

    def added(offset):
        return joined(wide[pl.ds(offset, piece), :])

    def apply_grams(picked, gather):
        columns = picked.T
        for slot in range(slots):
            column = jnp.broadcast_to(columns[:, slot : slot + 1], (128, 128))
            sums[slot * SUB : (slot + 1) * SUB, :] = jnp.sum(
                (grams[slot] * column).reshape(128 // SUB, SUB, 128), axis=0
            )
        total = sums[pl.ds(0, slots, stride=SUB), :]
        for part in range(1, SUB):
            total = total + sums[pl.ds(part, slots, stride=SUB), :]
        gather[orbit] = total
        return total

    one_copy(orbit, partner, 0).wait_recv()
    for step in x_steps:
        one_copy(orbit, partner, xs - 1 + step).wait_recv()
    learned(0, 2)
    for step in both_ways(4):
        signal(known.at[1], column_peer(step))

    matches = match[...].astype(BF16)
    diagonal = slot_rows(gather_one, slots)
    data = slot_rows(gather_one, 0)
    shifted = kap_picks[...] + 4.0
    diagonal_here = joined(jnp.dot(matches, halves(diagonal), preferred_element_type=F32))
    data_here = joined(jnp.dot(matches, halves(data), preferred_element_type=F32))
    inverse_here = 1.0 / (prior_weight * (shifted * shifted + 4.0) + diagonal_here)
    inverse_picks[...] = inverse_here
    apply_grams(data_here * inverse_here, gather_two)
    orbit_start(gather_two, 2)

    scatter(diagonal)

    def make_inverse(offset):
        shifted = kap_own[pl.ds(offset, piece), :] + 4.0
        inverse[pl.ds(offset, piece), :] = 1.0 / (prior_weight * (shifted * shifted + 4.0) + added(offset))

    each_piece(make_inverse)
    scatter(data)

    def make_z(offset):
        data_part = added(offset)
        right[pl.ds(offset, piece), :] = data_part
        scaled = data_part * inverse[pl.ds(offset, piece), :]
        z_own[pl.ds(offset, piece), :] = scaled
        z_ext[pl.ds(offset + 2 * SUB, piece), :] = scaled

    each_piece(make_z)

    z_halo = [
        halo_copy(z_own, rows - 2, z_ext, 0, 2, 1, 0, east),
        halo_copy(z_own, 0, z_ext, rows + 2, 2, 1, 1, west),
    ]
    for copy in z_halo:
        copy.start()
    for copy in kap_halo + z_halo:
        copy.wait_recv()

    first_rows = 6

    def first_stencil(ext):
        @pl.loop(0, (rows + 2) // first_rows)
        def _(step):
            row = step * first_rows
            k_ext[pl.ds(pl.multiple_of(row * SUB, SUB), first_rows * SUB), :] = stencil(
                ext, row + 1, kap, row, first_rows
            ).reshape(first_rows * SUB, 128)

    def second_stencil(target):
        @pl.loop(0, rows // SUB)
        def _(step):
            row = step * SUB
            target[pl.ds(pl.multiple_of(row * SUB, SUB), SUB * SUB), :] = prior_weight * stencil(
                k_ext, row + 1, kap, row + 1, SUB
            ).reshape(SUB * SUB, 128)

    first_stencil(z_ext)
    second_stencil(y_own)
    pick(y_own, picks)

    orbit_wait(gather_two, 2)
    terms = slot_rows(gather_two, 0)
    edge = 2 * SUB
    tail = tiles - edge
    ahead = jnp.concatenate([hot[0:edge], hot[tail:tiles], matches], axis=0)
    early = joined(jnp.dot(ahead, halves(terms), preferred_element_type=F32))
    w_edge[0:edge] = (y_own[0:edge] + early[0:edge]) * inverse[0:edge]
    w_edge[edge : 2 * edge] = (y_own[tail:tiles] + early[edge : 2 * edge]) * inverse[tail:tiles]
    w_halo = [
        halo_copy(w_edge, 2, w_ext, 0, 2, 2, 0, east),
        halo_copy(w_edge, 0, w_ext, rows + 2, 2, 2, 1, west),
    ]
    for copy in w_halo:
        copy.start()
    w_here = (picks[...] + early[2 * edge :]) * inverse_picks[...]
    w_terms = apply_grams(w_here, gather_three)
    last = jnp.sum((w_here * w_terms).reshape(slots // SUB, SUB, 128), axis=0)
    scatter(terms)

    def make_w(offset):
        part = pl.ds(offset, piece)
        image = y_own[part, :] + added(offset)
        y_own[part, :] = image
        scaled = image * inverse[part, :]
        w_own[part, :] = scaled
        w_ext[pl.ds(offset + 2 * SUB, piece), :] = scaled

    each_piece(make_w)

    share_rows = rows // orbits
    share_row = orbit * share_rows
    share = pl.ds(pl.multiple_of(share_row * SUB, SUB), share_rows * SUB)

    def folded(product):
        return jnp.sum(product.reshape(share_rows, SUB, 128), axis=0)

    products = [
        folded(right[share, :] * z_own[share, :]),
        folded(y_own[share, :] * z_own[share, :]),
        folded(y_own[share, :] * w_own[share, :]),
    ]
    for copy in w_halo:
        copy.wait_recv()
    own_k = stencil(w_ext, share_row + 2, kap, share_row + 1, share_rows)
    products.append(last + prior_weight * jnp.sum(own_k * own_k, axis=0))
    row_index = lax.broadcasted_iota(jnp.int32, (SUB, 128), 0)
    lane_index = lax.broadcasted_iota(jnp.int32, (SUB, 128), 1)
    stacked = jnp.zeros((SUB, 128), F32)
    for index, product in enumerate(products):
        stacked = jnp.where(row_index == index, jnp.sum(product, axis=0, keepdims=True), stacked)
    stacked = stacked + pltpu.roll(stacked, 64, axis=1)
    stacked = stacked + pltpu.roll(stacked, 32, axis=1)
    packed = jnp.sum(jnp.where(lane_index // 32 == row_index, stacked, 0.0), axis=0, keepdims=True)
    plane_stats[me_plane] = packed

    def plane_copy(step):
        return pltpu.make_async_remote_copy(
            src_ref=plane_stats.at[me_plane],
            dst_ref=plane_stats.at[me_plane],
            send_sem=plane_send.at[step],
            recv_sem=plane_recv.at[step],
            device_id=plane_peer(step),
            device_id_type=MESH,
        )

    def column_copy(step):
        return pltpu.make_async_remote_copy(
            src_ref=column_stats.at[z],
            dst_ref=column_stats.at[z],
            send_sem=column_send.at[step],
            recv_sem=column_recv.at[step],
            device_id=column_peer(step),
            device_id_type=MESH,
        )

    @pl.loop(1, plane)
    def _(step):
        plane_copy(step).start()

    orbit_start(gather_three, 3)
    first_stencil(w_ext)

    @pl.loop(1, plane)
    def _(step):
        plane_copy(step).wait_recv()

    total = plane_stats[0]
    for index in range(1, plane):
        total = total + plane_stats[index]
    column_stats[z] = total
    learned(1, 4)

    @pl.loop(1, zs)
    def _(step):
        column_copy(step).start()

    second_stencil(q_own)
    orbit_wait(gather_three, 3)
    scatter(slot_rows(gather_three, 0))

    def make_q(offset):
        part = pl.ds(offset, piece)
        q_own[part, :] = q_own[part, :] + added(offset)

    each_piece(make_q)

    @pl.loop(1, zs)
    def _(step):
        column_copy(step).wait_recv()

    total = column_stats[0]
    for index in range(1, zs):
        total = total + column_stats[index]
    g = [
        jnp.sum(jnp.where(lane_row // 32 == index, total, 0.0), axis=1, keepdims=True)
        for index in range(4)
    ]
    alpha = g[0] / g[1]
    later = alpha * alpha * g[2] - g[0]
    grow = 1.0 + later / g[0]
    alpha_later = later / (grow * grow * g[1] - 2.0 * grow * alpha * g[2] + alpha * alpha * g[3])
    on_first = alpha + alpha_later * grow
    on_second = alpha_later * alpha

    def finish(offset):
        part = pl.ds(offset, piece)
        w_own[part, :] = on_first * z_own[part, :] - on_second * w_own[part, :]
        q_own[part, :] = right[part, :] - on_first * y_own[part, :] + on_second * q_own[part, :]

    each_piece(finish)

    @pl.loop(0, rows // SUB)
    def _(group):
        for tile in range(SUB):
            strided = pl.ds(group * SUB * SUB + tile, SUB, stride=SUB)
            place = pl.ds(pl.multiple_of(group * SUB, SUB), SUB)
            out_solution[place, tile * 128 : (tile + 1) * 128] = w_own[strided, :]
            out_residual[place, tile * 128 : (tile + 1) * 128] = q_own[strided, :]

    for which, buffer in ((0, codes), (2, gather_two), (3, gather_three)):
        for step in range(1, orbits):
            orbit_copy(buffer, which, step).wait_send()
    for copy in own_copies + forwards + kap_halo + z_halo + w_halo:
        copy.wait_send()

    @pl.loop(1, plane)
    def _(step):
        plane_copy(step).wait_send()

    @pl.loop(1, zs)
    def _(step):
        column_copy(step).wait_send()


def solution(mesh):
    return build(mesh, 4, 16)


def build(mesh, ys, zs):
    orbits = mesh.shape["orbit"]

    def per_device(interp, obs_value, obs_weight, block_map, live_count, kappa2):
        slots, _, obs, cells = interp.shape
        rows, lat = kappa2.shape
        tiles = rows * lat // cells
        plane = orbits * ys
        hot_width = max(orbits * slots, 128)
        vmem = pltpu.VMEM
        field = vmem((tiles, 128), F32)
        extended = vmem((tiles + 4 * SUB, 128), F32)
        inner = vmem((tiles + 2 * SUB, 128), F32)
        gather = vmem((orbits, slots, 128), F32)
        return pl.pallas_call(
            functools.partial(kernel, (orbits, ys, zs)),
            out_shape=(
                pltpu.VMEM(kappa2.shape, F32),
                pltpu.VMEM(kappa2.shape, F32),
            ),
            in_specs=[pl.BlockSpec(memory_space=pltpu.HBM)] * 6,
            out_specs=(pl.BlockSpec(memory_space=vmem), pl.BlockSpec(memory_space=vmem)),
            scratch_shapes=[
                pltpu.SMEM((slots,), jnp.int32),
                pltpu.SMEM((1, 1), jnp.int32),
                vmem((slots, obs, cells), BF16),
                vmem((slots, 1, obs), F32),
                vmem((slots, 1, obs), F32),
                vmem((rows, lat), F32),
                field,
                inner,
                vmem((slots, 128, 128), F32),
                vmem((tiles, hot_width), BF16),
                vmem((slots, hot_width), F32),
                vmem((orbits, 1, 128), F32),
                vmem((orbits, 2 * slots, 128), F32),
                gather,
                gather,
                field,
                field,
                field,
                extended,
                inner,
                field,
                field,
                vmem((4 * SUB, 128), F32),
                extended,
                field,
                vmem((slots, 128), F32),
                vmem((slots, 128), F32),
                vmem((slots, 128), F32),
                vmem((slots * SUB, 128), F32),
                vmem((tiles, 256), F32),
                vmem((plane, 1, 128), F32),
                vmem((zs, 1, 128), F32),
                pltpu.SemaphoreType.DMA((5 + CHUNKS,)),
                pltpu.SemaphoreType.DMA((4, orbits)),
                pltpu.SemaphoreType.DMA((4, orbits)),
                pltpu.SemaphoreType.DMA((orbits,)),
                pltpu.SemaphoreType.DMA((orbits,)),
                pltpu.SemaphoreType.DMA((3, 2)),
                pltpu.SemaphoreType.DMA((3, 2)),
                pltpu.SemaphoreType.DMA((plane,)),
                pltpu.SemaphoreType.DMA((plane,)),
                pltpu.SemaphoreType.DMA((zs,)),
                pltpu.SemaphoreType.DMA((zs,)),
                pltpu.SemaphoreType.REGULAR((2,)),
            ],
            compiler_params=pltpu.CompilerParams(
                collective_id=0, has_side_effects=True, vmem_limit_bytes=66400000
            ),
        )(
            interp.reshape(slots, obs, cells),
            obs_value,
            obs_weight,
            block_map.reshape(slots),
            live_count,
            kappa2,
        )

    in_specs = (
        P("orbit", "lon", None, None),
        P("orbit", "lon", None),
        P("orbit", "lon", None),
        P("orbit", "lon"),
        P("orbit", "lon"),
        P("lon", None),
    )
    out_specs = (P("lon", None), P("lon", None))
    return jax.shard_map(
        per_device, mesh=mesh, in_specs=in_specs, out_specs=out_specs, check_vma=False
    )
```

```python
import functools

import jax
import jax.numpy as jnp
from jax import lax
from jax.experimental import pallas as pl
from jax.experimental.pallas import tpu as pltpu
from jax.sharding import PartitionSpec as P

MESH = pl.DeviceIdType.MESH
F32 = jnp.float32
BF16 = jnp.bfloat16

prior_weight = 0.0625
SUB = 8
CHUNKS = 4
SPLIT = (12, 24)
SPLIT_OF = 32


def split(value):
    high = value.astype(BF16)
    return high, (value - high.astype(F32)).astype(BF16)


def tree_sum(values):
    while len(values) > 1:
        values = [sum(values[at : at + 2][1:], values[at]) for at in range(0, len(values), 2)]
    return values[0]


def lat_pair(cells, lane, sub):
    up = pltpu.roll(cells, 127, axis=2)
    down = pltpu.roll(cells, 1, axis=2)
    up_edge = jnp.where(sub == SUB - 1, 0.0, pltpu.roll(up, SUB - 1, axis=1))
    down_edge = jnp.where(sub == 0, 0.0, pltpu.roll(down, 1, axis=1))
    return jnp.where(lane == 127, up_edge, up) + jnp.where(lane == 0, down_edge, down)


def stencil(source, source_row, kappa, kappa_row, rows):
    shape = (rows, SUB, 128)
    lane = lax.broadcasted_iota(jnp.int32, shape, 2)
    sub = lax.broadcasted_iota(jnp.int32, shape, 1)

    def part(ref, row):
        return ref[pl.ds(pl.multiple_of(row * SUB, SUB), rows * SUB), :].reshape(shape)

    center = part(source, source_row)
    around = part(source, source_row + 1) + part(source, source_row - 1)
    return (part(kappa, kappa_row) + 4.0) * center - around - lat_pair(center, lane, sub)


def kernel(
    dims, interp, value, weight, targets_hbm, count_hbm, kappa, out_z, out_w, out_right, out_y, out_q, out_first, out_second,
    targets, count, blocks, values, weights, kappa_in, kap_own, kap, grams, hot, match,
    codes, gather_one, gather_two, gather_three,
    right, inverse, z_own, z_edge, z_ext, k_ext, y_own, w_own, w_edge, w_ext, q_own,
    kap_picks, inverse_picks, picks, wide, plane_stats, column_stats,
    load_sem, orbit_send, orbit_recv, one_send, one_recv, halo_send, halo_recv,
    plane_send, plane_recv, column_send, column_recv, known,
):
    orbits, ys, zs = dims
    xs = orbits // 2
    slots = weights.shape[0]
    obs = weights.shape[2]
    rows = kappa_in.shape[0]
    tiles = rows * SUB
    plane = orbits * ys
    lons = ys * zs
    orbit = lax.axis_index("orbit")
    lon = lax.axis_index("lon")
    x = orbit // 2
    core = lax.rem(orbit, 2)
    y = lon // zs
    z = lax.rem(lon, zs)
    east = lax.rem(lon + 1, lons)
    west = lax.rem(lon + lons - 1, lons)
    me_plane = orbit * ys + y

    per_chunk = slots // CHUNKS
    load_t = pltpu.make_async_copy(targets_hbm, targets, load_sem.at[3 + CHUNKS])
    load_c = pltpu.make_async_copy(count_hbm, count, load_sem.at[4 + CHUNKS])
    load_w = pltpu.make_async_copy(weight, weights, load_sem.at[0])
    load_v = pltpu.make_async_copy(value, values, load_sem.at[1])
    load_k = pltpu.make_async_copy(kappa, kappa_in, load_sem.at[2])
    load_w.start()
    load_v.start()
    loads = []
    for chunk in range(CHUNKS):
        part = pl.ds(chunk * per_chunk, per_chunk)
        loads.append(pltpu.make_async_copy(interp.at[part], blocks.at[part], load_sem.at[3 + chunk]))
        loads[-1].start()
    load_t.start()
    load_c.start()
    load_k.start()

    def plane_peer(step):
        there = lax.rem(me_plane + step, plane)
        return (there // ys, lax.rem(there, ys) * zs + z)

    def column_peer(step):
        return (orbit, y * zs + lax.rem(z + step, zs))

    def signal(semaphore, device):
        pl.semaphore_signal(semaphore, inc=1, device_id=device, device_id_type=MESH)

    def both_ways(step):
        return sorted({step % zs, -step % zs} - {0})

    def learned(which, step):
        if both_ways(step):
            pl.semaphore_wait(known.at[which], len(both_ways(step)))

    barrier = pltpu.get_barrier_semaphore()
    near = [(lax.rem(orbit + step, orbits), lon) for step in range(1, orbits)]
    near += [(orbit, lax.rem(y + step, ys) * zs + z) for step in range(1, ys)]
    near += [column_peer(step) for step in sorted({1 % zs, -1 % zs, 2 % zs, -2 % zs} - {0})]
    near += [(orbit, east), (orbit, west)]
    for device in near:
        signal(barrier, device)

    load_w.wait()
    load_v.wait()
    load_c.wait()
    live = count[0, 0]
    first_row = lax.broadcasted_iota(jnp.int32, (16, obs), 0) == 0
    for chunk in range(CHUNKS):
        loads[chunk].wait()

        @pl.loop(chunk * per_chunk, (chunk + 1) * per_chunk, unroll=per_chunk)
        def _(slot):
            block = blocks[slot]
            weight_row = weights[slot]
            left = jnp.where(first_row, weight_row * values[slot], weight_row).astype(BF16)
            product = jnp.dot(
                left, jnp.concatenate([block, block * block], axis=1), preferred_element_type=F32
            )
            factor = jnp.where(slot < live, 1.0, 0.0)
            gather_one[orbit, pl.ds(slot, 1), :] = product[0:1, :128] * factor
            gather_one[orbit, pl.ds(slots + slot, 1), :] = product[1:2, 128:] * factor

    load_t.wait()
    lane_row = lax.broadcasted_iota(jnp.int32, (1, 128), 1)
    first_lane = lax.rem(orbit, 128 // slots) * slots
    code = jnp.zeros((1, 128), jnp.int32)
    for slot in range(slots):
        code = jnp.where(lane_row == first_lane + slot, targets[slot] + 1, code)
    code = jnp.where(lane_row - first_lane < live, code, 0)
    codes[orbit] = code.astype(F32)

    pl.semaphore_wait(barrier, len(near))

    def orbit_copy(buffer, which, step):
        return pltpu.make_async_remote_copy(
            src_ref=buffer.at[orbit],
            dst_ref=buffer.at[orbit],
            send_sem=orbit_send.at[which, step],
            recv_sem=orbit_recv.at[which, step],
            device_id=(lax.rem(orbit + step, orbits), lon),
            device_id_type=MESH,
        )

    def orbit_start(buffer, which):
        for step in range(1, orbits):
            orbit_copy(buffer, which, step).start()

    def orbit_wait(buffer, which):
        for step in range(1, orbits):
            orbit_copy(buffer, which, step).wait_recv()

    def one_copy(owner, device, index):
        return pltpu.make_async_remote_copy(
            src_ref=gather_one.at[owner],
            dst_ref=gather_one.at[owner],
            send_sem=one_send.at[index],
            recv_sem=one_recv.at[index],
            device_id=(device, lon),
            device_id_type=MESH,
        )

    def along(step):
        return lax.rem(x + step + xs, xs) * 2 + core

    partner = x * 2 + 1 - core
    x_steps = sorted(range(1, xs), key=lambda step: min(step, xs - step))
    own_copies = [one_copy(orbit, along(step), step) for step in reversed(x_steps)]
    own_copies.append(one_copy(orbit, partner, 0))
    for copy in own_copies:
        copy.start()
    orbit_start(codes, 0)
    for step in both_ways(2):
        signal(known.at[0], column_peer(step))

    def halo_copy(source, source_row, target, target_row, count_rows, which, side, device):
        return pltpu.make_async_remote_copy(
            src_ref=source.at[pl.ds(source_row * SUB, count_rows * SUB)],
            dst_ref=target.at[pl.ds(target_row * SUB, count_rows * SUB)],
            send_sem=halo_send.at[which, side],
            recv_sem=halo_recv.at[which, side],
            device_id=(orbit, device),
            device_id_type=MESH,
        )

    load_k.wait()

    @pl.loop(0, rows // SUB, unroll=2)
    def _(group):
        for tile in range(SUB):
            values_here = kappa_in[
                pl.ds(pl.multiple_of(group * SUB, SUB), SUB), tile * 128 : (tile + 1) * 128
            ]
            kap[pl.ds((group * SUB + 1) * SUB + tile, SUB, stride=SUB), :] = values_here
            kap_own[pl.ds(group * SUB * SUB + tile, SUB, stride=SUB), :] = values_here

    kap_halo = [
        halo_copy(kap_own, rows - 1, kap, 0, 1, 0, 0, east),
        halo_copy(kap_own, 0, kap, rows + 1, 1, 0, 1, west),
    ]
    for copy in kap_halo:
        copy.start()

    def pick(own, target):
        for slot in range(slots):
            target[slot : slot + 1, :] = own[pl.ds(targets[slot], 1), :]

    pick(kap_own, kap_picks)

    def halves(terms):
        return jnp.concatenate(split(terms), axis=1)

    def joined(product):
        return product[:, :128] + product[:, 128:]

    def make_grams(begin, end):
        @pl.loop(begin, end, unroll=4)
        def _(slot):
            block = blocks[slot]
            left = (block.T.astype(F32) * weights[slot]).astype(BF16)
            product = jnp.dot(left, block, preferred_element_type=F32)
            grams[slot] = halves(product * jnp.where(slot < live, 1.0, 0.0))

    forwards = []

    def forward(step):
        one_copy(orbit, along(step), step).wait_recv()
        forwards.append(one_copy(along(-step), partner, xs - 1 + step))
        forwards[-1].start()

    cuts = [0] + [slots * part // SPLIT_OF for part in SPLIT] + [slots]
    make_grams(cuts[0], cuts[1])

    orbit_wait(codes, 0)
    groups = hot.shape[1] // 128
    per_group = orbits // groups
    for group in range(groups):
        row = codes[group * per_group]
        for member in range(1, per_group):
            row = row + codes[group * per_group + member]
        part = 64
        columns = slice(group * 128, (group + 1) * 128)
        for slot in range(slots):
            wanted = (targets[slot] + 1).astype(F32)
            match[slot : slot + 1, columns] = jnp.where(row == wanted, 1.0, 0.0)

        @pl.loop(0, tiles // part, unroll=4)
        def _(step):
            offset = pl.multiple_of(step * part, part)
            cell = lax.broadcasted_iota(jnp.int32, (part, 128), 0) + (offset + 1)
            hot[pl.ds(offset, part), columns] = jnp.where(cell.astype(F32) == row, 1.0, 0.0).astype(BF16)

    for step in x_steps[:2]:
        forward(step)
    make_grams(cuts[1], cuts[2])
    for step in x_steps[2:]:
        forward(step)
    make_grams(cuts[2], cuts[3])

    def scatter(terms):
        wide[...] = jnp.dot(hot[...], halves(terms), preferred_element_type=F32)

    def slot_rows(buffer, first):
        return buffer[:, first : first + slots, :].reshape(orbits * slots, 128)

    piece = 8 * SUB

    def each_piece(body):
        @pl.loop(0, tiles // piece, unroll=4)
        def _(step):
            body(pl.multiple_of(step * piece, piece))

    def added(offset):
        return joined(wide[pl.ds(offset, piece), :])

    sub_index = lax.broadcasted_iota(jnp.int32, (SUB, 128), 0)
    even = lax.rem(sub_index, 2) == 0

    def apply_grams(picked, gather):
        results = []
        for first in range(0, slots, SUB):
            rows_here = picked[first : first + SUB]
            high = rows_here.astype(BF16).astype(F32)
            stack = jnp.concatenate([high, rows_here - high], axis=0)
            both = jnp.concatenate([even, even], axis=0)
            left = jnp.concatenate(
                [jnp.where(both, stack, 0.0), jnp.where(both, 0.0, stack)], axis=1
            ).astype(BF16)
            result = None
            for pair in range(SUB // 2):
                slot = first + 2 * pair
                product = jnp.dot(
                    left, grams[slot : slot + 2].reshape(256, 256), preferred_element_type=F32
                )
                product = joined(product)
                product = product[:SUB] + product[SUB:]
                result = product if result is None else jnp.where(sub_index // 2 == pair, product, result)
            results.append(result)
        total = jnp.concatenate(results, axis=0)
        gather[orbit] = total
        return total

    one_copy(orbit, partner, 0).wait_recv()
    for step in x_steps:
        one_copy(orbit, partner, xs - 1 + step).wait_recv()
    learned(0, 2)
    for step in both_ways(4):
        signal(known.at[1], column_peer(step))

    edge = 2 * SUB
    tail = tiles - edge
    ahead = jnp.concatenate([hot[0:edge], hot[tail:tiles], match[...].astype(BF16)], axis=0)

    def early(terms):
        return joined(jnp.dot(ahead, halves(terms), preferred_element_type=F32))

    def inverse_of(kappa_part, diagonal_part):
        shifted = kappa_part + 4.0
        return 1.0 / (prior_weight * (shifted * shifted + 4.0) + diagonal_part)

    diagonal = slot_rows(gather_one, slots)
    data = slot_rows(gather_one, 0)
    kap_ahead = jnp.concatenate([kap_own[0:edge], kap_own[tail:tiles], kap_picks[...]], axis=0)
    inverse_ahead = inverse_of(kap_ahead, early(diagonal))
    z_ahead = early(data) * inverse_ahead
    z_edge[...] = z_ahead[: 2 * edge]
    z_halo = [
        halo_copy(z_edge, 2, z_ext, 0, 2, 1, 0, east),
        halo_copy(z_edge, 0, z_ext, rows + 2, 2, 1, 1, west),
    ]
    for copy in z_halo:
        copy.start()
    inverse_picks[...] = inverse_ahead[2 * edge :]
    apply_grams(z_ahead[2 * edge :], gather_two)
    orbit_start(gather_two, 2)

    scatter(diagonal)

    def make_inverse(offset):
        part = pl.ds(offset, piece)
        inverse[part, :] = inverse_of(kap_own[part, :], added(offset))

    each_piece(make_inverse)
    scatter(data)

    def make_z(offset):
        data_part = added(offset)
        right[pl.ds(offset, piece), :] = data_part
        scaled = data_part * inverse[pl.ds(offset, piece), :]
        z_own[pl.ds(offset, piece), :] = scaled
        z_ext[pl.ds(offset + 2 * SUB, piece), :] = scaled

    each_piece(make_z)

    for copy in kap_halo + z_halo:
        copy.wait_recv()

    first_rows = 11

    def first_stencil(ext):
        @pl.loop(0, (rows + 2) // first_rows, unroll=2)
        def _(step):
            row = step * first_rows
            k_ext[pl.ds(pl.multiple_of(row * SUB, SUB), first_rows * SUB), :] = stencil(
                ext, row + 1, kap, row, first_rows
            ).reshape(first_rows * SUB, 128)

    def second_stencil(target):
        @pl.loop(0, rows // SUB, unroll=2)
        def _(step):
            row = step * SUB
            target[pl.ds(pl.multiple_of(row * SUB, SUB), SUB * SUB), :] = prior_weight * stencil(
                k_ext, row + 1, kap, row + 1, SUB
            ).reshape(SUB * SUB, 128)

    first_stencil(z_ext)
    second_stencil(y_own)
    pick(y_own, picks)

    orbit_wait(gather_two, 2)
    terms = slot_rows(gather_two, 0)
    terms_ahead = early(terms)
    y_ahead = jnp.concatenate([y_own[0:edge], y_own[tail:tiles], picks[...]], axis=0)
    inverse_ahead = jnp.concatenate([inverse[0:edge], inverse[tail:tiles], inverse_picks[...]], axis=0)
    w_ahead = (y_ahead + terms_ahead) * inverse_ahead
    w_edge[...] = w_ahead[: 2 * edge]
    w_halo = [
        halo_copy(w_edge, 2, w_ext, 0, 2, 2, 0, east),
        halo_copy(w_edge, 0, w_ext, rows + 2, 2, 2, 1, west),
    ]
    for copy in w_halo:
        copy.start()
    w_here = w_ahead[2 * edge :]
    w_terms = apply_grams(w_here, gather_three)
    last = jnp.sum((w_here * w_terms).reshape(slots // SUB, SUB, 128), axis=0)
    scatter(terms)

    def make_w(offset):
        part = pl.ds(offset, piece)
        image = y_own[part, :] + added(offset)
        y_own[part, :] = image
        scaled = image * inverse[part, :]
        w_own[part, :] = scaled
        w_ext[pl.ds(offset + 2 * SUB, piece), :] = scaled

    each_piece(make_w)

    share_rows = rows // orbits
    share_row = orbit * share_rows
    share = pl.ds(pl.multiple_of(share_row * SUB, SUB), share_rows * SUB)

    def folded(product):
        return jnp.sum(product.reshape(share_rows, SUB, 128), axis=0)

    products = [
        folded(right[share, :] * z_own[share, :]),
        folded(y_own[share, :] * z_own[share, :]),
        folded(y_own[share, :] * w_own[share, :]),
    ]
    for copy in w_halo:
        copy.wait_recv()
    own_k = stencil(w_ext, share_row + 2, kap, share_row + 1, share_rows)
    products.append(last + prior_weight * jnp.sum(own_k * own_k, axis=0))
    lane_index = lax.broadcasted_iota(jnp.int32, (SUB, 128), 1)
    stacked = jnp.zeros((SUB, 128), F32)
    for index, product in enumerate(products):
        stacked = jnp.where(sub_index == index, jnp.sum(product, axis=0, keepdims=True), stacked)
    stacked = stacked + pltpu.roll(stacked, 64, axis=1)
    stacked = stacked + pltpu.roll(stacked, 32, axis=1)
    packed = jnp.sum(jnp.where(lane_index // 32 == sub_index, stacked, 0.0), axis=0, keepdims=True)
    plane_stats[me_plane] = packed

    def plane_copy(step):
        return pltpu.make_async_remote_copy(
            src_ref=plane_stats.at[me_plane],
            dst_ref=plane_stats.at[me_plane],
            send_sem=plane_send.at[step],
            recv_sem=plane_recv.at[step],
            device_id=plane_peer(step),
            device_id_type=MESH,
        )

    def column_copy(step):
        return pltpu.make_async_remote_copy(
            src_ref=column_stats.at[z],
            dst_ref=column_stats.at[z],
            send_sem=column_send.at[step],
            recv_sem=column_recv.at[step],
            device_id=column_peer(step),
            device_id_type=MESH,
        )

    for step in range(1, plane):
        plane_copy(step).start()

    orbit_start(gather_three, 3)

    def lay_out(source, target):
        @pl.loop(0, rows // SUB, unroll=2)
        def _(group):
            for tile in range(SUB):
                place = pl.ds(pl.multiple_of(group * SUB, SUB), SUB)
                target[place, tile * 128 : (tile + 1) * 128] = source[
                    pl.ds(group * SUB * SUB + tile, SUB, stride=SUB), :
                ]

    first_stencil(w_ext)
    lay_out(z_own, out_z)
    lay_out(right, out_right)
    lay_out(y_own, out_y)
    lay_out(w_own, out_w)

    @pl.loop(1, plane)
    def _(step):
        plane_copy(step).wait_recv()

    total = tree_sum([plane_stats[index] for index in range(plane)])
    column_stats[z] = total
    learned(1, 4)

    for step in range(1, zs):
        column_copy(step).start()

    second_stencil(q_own)
    orbit_wait(gather_three, 3)
    scatter(slot_rows(gather_three, 0))

    def make_q(offset):
        part = pl.ds(offset, piece)
        q_own[part, :] = q_own[part, :] + added(offset)

    each_piece(make_q)
    lay_out(q_own, out_q)

    for which, buffer in ((0, codes), (2, gather_two), (3, gather_three)):
        for step in range(1, orbits):
            orbit_copy(buffer, which, step).wait_send()
    for copy in own_copies + forwards + kap_halo + z_halo + w_halo:
        copy.wait_send()

    @pl.loop(1, plane)
    def _(step):
        plane_copy(step).wait_send()

    @pl.loop(1, zs)
    def _(step):
        column_copy(step).wait_send()

    @pl.loop(1, zs)
    def _(step):
        column_copy(step).wait_recv()

    total = tree_sum([column_stats[index] for index in range(zs)])
    g = [
        jnp.sum(jnp.where(lane_row // 32 == index, total, 0.0), axis=1, keepdims=True)
        for index in range(4)
    ]
    alpha = g[0] / g[1]
    later = alpha * alpha * g[2] - g[0]
    grow = 1.0 + later / g[0]
    alpha_later = later / (grow * grow * g[1] - 2.0 * grow * alpha * g[2] + alpha * alpha * g[3])
    on_first = alpha + alpha_later * grow
    on_second = alpha_later * alpha

    out_first[...] = on_first
    out_second[...] = on_second


def solution(mesh):
    return build(mesh, 4, 16)


def build(mesh, ys, zs):
    orbits = mesh.shape["orbit"]

    def per_device(interp, obs_value, obs_weight, block_map, live_count, kappa2):
        slots, _, obs, cells = interp.shape
        rows, lat = kappa2.shape
        tiles = rows * lat // cells
        plane = orbits * ys
        hot_width = max(orbits * slots, 128)
        vmem = pltpu.VMEM
        field = vmem((tiles, 128), F32)
        extended = vmem((tiles + 4 * SUB, 128), F32)
        inner = vmem((tiles + 2 * SUB, 128), F32)
        gather = vmem((orbits, slots, 128), F32)
        z, w, right, y, q, on_first, on_second = pl.pallas_call(
            functools.partial(kernel, (orbits, ys, zs)),
            out_shape=(
                *([pltpu.VMEM(kappa2.shape, F32)] * 5),
                *([pltpu.VMEM((1, 1), F32)] * 2),
            ),
            in_specs=[pl.BlockSpec(memory_space=pltpu.HBM)] * 6,
            out_specs=(pl.BlockSpec(memory_space=vmem),) * 7,
            scratch_shapes=[
                pltpu.SMEM((slots,), jnp.int32),
                pltpu.SMEM((1, 1), jnp.int32),
                vmem((slots, obs, cells), BF16),
                vmem((slots, 1, obs), F32),
                vmem((slots, 1, obs), F32),
                vmem((rows, lat), F32),
                field,
                inner,
                vmem((slots, 128, 256), BF16),
                vmem((tiles, hot_width), BF16),
                vmem((slots, hot_width), F32),
                vmem((orbits, 1, 128), F32),
                vmem((orbits, 2 * slots, 128), F32),
                gather,
                gather,
                field,
                field,
                field,
                vmem((4 * SUB, 128), F32),
                extended,
                inner,
                field,
                field,
                vmem((4 * SUB, 128), F32),
                extended,
                field,
                vmem((slots, 128), F32),
                vmem((slots, 128), F32),
                vmem((slots, 128), F32),
                vmem((tiles, 256), F32),
                vmem((plane, 1, 128), F32),
                vmem((zs, 1, 128), F32),
                pltpu.SemaphoreType.DMA((5 + CHUNKS,)),
                pltpu.SemaphoreType.DMA((4, orbits)),
                pltpu.SemaphoreType.DMA((4, orbits)),
                pltpu.SemaphoreType.DMA((orbits,)),
                pltpu.SemaphoreType.DMA((orbits,)),
                pltpu.SemaphoreType.DMA((3, 2)),
                pltpu.SemaphoreType.DMA((3, 2)),
                pltpu.SemaphoreType.DMA((plane,)),
                pltpu.SemaphoreType.DMA((plane,)),
                pltpu.SemaphoreType.DMA((zs,)),
                pltpu.SemaphoreType.DMA((zs,)),
                pltpu.SemaphoreType.REGULAR((2,)),
            ],
            compiler_params=pltpu.CompilerParams(
                collective_id=0, has_side_effects=True, vmem_limit_bytes=65600000
            ),
        )(
            interp.reshape(slots, obs, cells),
            obs_value,
            obs_weight,
            block_map.reshape(slots),
            live_count,
            kappa2,
        )
        on_first, on_second = on_first.reshape(()), on_second.reshape(())
        return on_first * z - on_second * w, right - on_first * y + on_second * q

    in_specs = (
        P("orbit", "lon", None, None),
        P("orbit", "lon", None),
        P("orbit", "lon", None),
        P("orbit", "lon"),
        P("orbit", "lon"),
        P("lon", None),
    )
    out_specs = (P("lon", None), P("lon", None))
    return jax.shard_map(
        per_device, mesh=mesh, in_specs=in_specs, out_specs=out_specs, check_vma=False
    )
```

```python
import functools

import jax
import jax.numpy as jnp
from jax import lax
from jax.experimental import pallas as pl
from jax.experimental.pallas import tpu as pltpu
from jax.sharding import PartitionSpec as P

MESH = pl.DeviceIdType.MESH
F32 = jnp.float32
BF16 = jnp.bfloat16

prior_weight = 0.0625
SUB = 8
CHUNKS = 4
SPLIT = (16, 24)
SPLIT_OF = 32


def split(value):
    high = value.astype(BF16)
    return high, (value - high.astype(F32)).astype(BF16)


def tree_sum(values):
    while len(values) > 1:
        values = [sum(values[at : at + 2][1:], values[at]) for at in range(0, len(values), 2)]
    return values[0]


def lat_pair(cells, lane, sub):
    up = pltpu.roll(cells, 127, axis=2)
    down = pltpu.roll(cells, 1, axis=2)
    up_edge = jnp.where(sub == SUB - 1, 0.0, pltpu.roll(up, SUB - 1, axis=1))
    down_edge = jnp.where(sub == 0, 0.0, pltpu.roll(down, 1, axis=1))
    return jnp.where(lane == 127, up_edge, up) + jnp.where(lane == 0, down_edge, down)


def stencil(source, source_row, kappa, kappa_row, rows):
    shape = (rows, SUB, 128)
    lane = lax.broadcasted_iota(jnp.int32, shape, 2)
    sub = lax.broadcasted_iota(jnp.int32, shape, 1)

    def part(ref, row):
        return ref[pl.ds(pl.multiple_of(row * SUB, SUB), rows * SUB), :].reshape(shape)

    center = part(source, source_row)
    around = part(source, source_row + 1) + part(source, source_row - 1)
    return (part(kappa, kappa_row) + 4.0) * center - around - lat_pair(center, lane, sub)


def kernel(
    dims, interp, value, weight, targets_hbm, count_hbm, kappa, out_z, out_w, out_right, out_y, out_q, out_first, out_second,
    targets, count, blocks, values, weights, kappa_in, kap_own, kap, grams, hot, match,
    codes, gather_one, gather_two, gather_three,
    right, inverse, z_own, z_edge, z_ext, k_ext, y_own, w_own, w_edge, w_land, w_ext, q_own,
    kap_picks, inverse_picks, picks, wide, plane_stats, cross_stats, column_stats,
    load_sem, orbit_send, orbit_recv, one_send, one_recv, halo_send, halo_recv,
    plane_send, plane_recv, cross_send, cross_recv, column_send, column_recv, known,
):
    orbits, ys, zs = dims
    xs = orbits // 2
    slots = weights.shape[0]
    obs = weights.shape[2]
    rows = kappa_in.shape[0]
    tiles = rows * SUB
    plane = orbits * ys
    lons = ys * zs
    orbit = lax.axis_index("orbit")
    lon = lax.axis_index("lon")
    x = orbit // 2
    core = lax.rem(orbit, 2)
    y = lon // zs
    z = lax.rem(lon, zs)
    east = lax.rem(lon + 1, lons)
    west = lax.rem(lon + lons - 1, lons)
    me_plane = orbit * ys + y

    per_chunk = slots // CHUNKS
    load_t = pltpu.make_async_copy(targets_hbm, targets, load_sem.at[3 + CHUNKS])
    load_c = pltpu.make_async_copy(count_hbm, count, load_sem.at[4 + CHUNKS])
    load_w = pltpu.make_async_copy(weight, weights, load_sem.at[0])
    load_v = pltpu.make_async_copy(value, values, load_sem.at[1])
    load_k = pltpu.make_async_copy(kappa, kappa_in, load_sem.at[2])
    load_w.start()
    load_v.start()
    loads = []
    for chunk in range(CHUNKS):
        part = pl.ds(chunk * per_chunk, per_chunk)
        loads.append(pltpu.make_async_copy(interp.at[part], blocks.at[part], load_sem.at[3 + chunk]))
        loads[-1].start()
    load_t.start()
    load_c.start()
    load_k.start()

    def plane_peer(step):
        there = lax.rem(me_plane + step, plane)
        return (there // ys, lax.rem(there, ys) * zs + z)

    def column_peer(step):
        return (orbit, y * zs + lax.rem(z + step, zs))

    def signal(semaphore, device):
        pl.semaphore_signal(semaphore, inc=1, device_id=device, device_id_type=MESH)

    def both_ways(step):
        return sorted({step % zs, -step % zs} - {0})

    def learned(which, step):
        if both_ways(step):
            pl.semaphore_wait(known.at[which], len(both_ways(step)))

    barrier = pltpu.get_barrier_semaphore()
    near = [(lax.rem(orbit + step, orbits), lon) for step in range(1, orbits)]
    near += [(orbit, lax.rem(y + step, ys) * zs + z) for step in range(1, ys)]
    near += [column_peer(step) for step in sorted({1 % zs, -1 % zs, 2 % zs, -2 % zs} - {0})]
    near += [(orbit, east), (orbit, west)]
    for device in near:
        signal(barrier, device)

    load_w.wait()
    load_v.wait()
    load_c.wait()
    live = count[0, 0]
    first_row = lax.broadcasted_iota(jnp.int32, (16, obs), 0) == 0
    for chunk in range(CHUNKS):
        loads[chunk].wait()

        @pl.loop(chunk * per_chunk, (chunk + 1) * per_chunk, unroll=per_chunk)
        def _(slot):
            block = blocks[slot]
            weight_row = weights[slot]
            left = jnp.where(first_row, weight_row * values[slot], weight_row).astype(BF16)
            product = jnp.dot(
                left, jnp.concatenate([block, block * block], axis=1), preferred_element_type=F32
            )
            factor = jnp.where(slot < live, 1.0, 0.0)
            gather_one[orbit, pl.ds(slot, 1), :] = product[0:1, :128] * factor
            gather_one[orbit, pl.ds(slots + slot, 1), :] = product[1:2, 128:] * factor

    load_t.wait()
    lane_row = lax.broadcasted_iota(jnp.int32, (1, 128), 1)
    first_lane = lax.rem(orbit, 128 // slots) * slots
    code = jnp.zeros((1, 128), jnp.int32)
    for slot in range(slots):
        code = jnp.where(lane_row == first_lane + slot, targets[slot] + 1, code)
    code = jnp.where(lane_row - first_lane < live, code, 0)
    codes[orbit] = code.astype(F32)

    pl.semaphore_wait(barrier, len(near))

    def orbit_copy(buffer, which, step):
        return pltpu.make_async_remote_copy(
            src_ref=buffer.at[orbit],
            dst_ref=buffer.at[orbit],
            send_sem=orbit_send.at[which, step],
            recv_sem=orbit_recv.at[which, step],
            device_id=(lax.rem(orbit + step, orbits), lon),
            device_id_type=MESH,
        )

    def orbit_start(buffer, which):
        for step in sorted(range(1, orbits), key=lambda step: -min(step, orbits - step)):
            orbit_copy(buffer, which, step).start()

    def orbit_wait(buffer, which):
        for step in range(1, orbits):
            orbit_copy(buffer, which, step).wait_recv()

    def one_copy(owner, device, index):
        return pltpu.make_async_remote_copy(
            src_ref=gather_one.at[owner],
            dst_ref=gather_one.at[owner],
            send_sem=one_send.at[index],
            recv_sem=one_recv.at[index],
            device_id=(device, lon),
            device_id_type=MESH,
        )

    def along(step):
        return lax.rem(x + step + xs, xs) * 2 + core

    partner = x * 2 + 1 - core
    x_steps = sorted(range(1, xs), key=lambda step: min(step, xs - step))
    own_copies = [one_copy(orbit, along(step), step) for step in reversed(x_steps)]
    own_copies.append(one_copy(orbit, partner, 0))
    orbit_start(codes, 0)
    for copy in own_copies:
        copy.start()
    for step in both_ways(2):
        signal(known.at[0], column_peer(step))

    def halo_copy(source, source_row, target, target_row, count_rows, which, side, device):
        return pltpu.make_async_remote_copy(
            src_ref=source.at[pl.ds(source_row * SUB, count_rows * SUB)],
            dst_ref=target.at[pl.ds(target_row * SUB, count_rows * SUB)],
            send_sem=halo_send.at[which, side],
            recv_sem=halo_recv.at[which, side],
            device_id=(orbit, device),
            device_id_type=MESH,
        )

    load_k.wait()

    @pl.loop(0, rows // SUB, unroll=2)
    def _(group):
        for tile in range(SUB):
            values_here = kappa_in[
                pl.ds(pl.multiple_of(group * SUB, SUB), SUB), tile * 128 : (tile + 1) * 128
            ]
            kap[pl.ds((group * SUB + 1) * SUB + tile, SUB, stride=SUB), :] = values_here
            kap_own[pl.ds(group * SUB * SUB + tile, SUB, stride=SUB), :] = values_here

    kap_halo = [
        halo_copy(kap_own, rows - 1, kap, 0, 1, 0, 0, east),
        halo_copy(kap_own, 0, kap, rows + 1, 1, 0, 1, west),
    ]
    for copy in kap_halo:
        copy.start()

    def pick(own, target):
        for slot in range(slots):
            target[slot : slot + 1, :] = own[pl.ds(targets[slot], 1), :]

    pick(kap_own, kap_picks)

    def halves(terms):
        return jnp.concatenate(split(terms), axis=1)

    def joined(product):
        return product[:, :128] + product[:, 128:]

    def make_grams(begin, end):
        @pl.loop(begin, end, unroll=4)
        def _(slot):
            block = blocks[slot]
            left = (block.T.astype(F32) * weights[slot]).astype(BF16)
            product = jnp.dot(left, block, preferred_element_type=F32)
            grams[slot] = halves(product * jnp.where(slot < live, 1.0, 0.0))

    forwards = []

    def forward(step):
        one_copy(orbit, along(step), step).wait_recv()
        forwards.append(one_copy(along(-step), partner, xs - 1 + step))
        forwards[-1].start()

    cuts = [0] + [slots * part // SPLIT_OF for part in SPLIT] + [slots]
    make_grams(cuts[0], cuts[1])

    orbit_wait(codes, 0)
    groups = hot.shape[1] // 128
    per_group = orbits // groups
    for group in range(groups):
        row = codes[group * per_group]
        for member in range(1, per_group):
            row = row + codes[group * per_group + member]
        part = 64
        columns = slice(group * 128, (group + 1) * 128)
        for slot in range(slots):
            wanted = (targets[slot] + 1).astype(F32)
            match[slot : slot + 1, columns] = jnp.where(row == wanted, 1.0, 0.0)

        @pl.loop(0, tiles // part, unroll=4)
        def _(step):
            offset = pl.multiple_of(step * part, part)
            cell = lax.broadcasted_iota(jnp.int32, (part, 128), 0) + (offset + 1)
            hot[pl.ds(offset, part), columns] = jnp.where(cell.astype(F32) == row, 1.0, 0.0).astype(BF16)

    for step in x_steps[:2]:
        forward(step)
    make_grams(cuts[1], cuts[2])
    for step in x_steps[2:]:
        forward(step)
    make_grams(cuts[2], cuts[3])

    def scatter(terms):
        wide[...] = jnp.dot(hot[...], halves(terms), preferred_element_type=F32)

    def slot_rows(buffer, first):
        return buffer[:, first : first + slots, :].reshape(orbits * slots, 128)

    piece = 8 * SUB

    def each_piece(body):
        @pl.loop(0, tiles // piece, unroll=4)
        def _(step):
            body(pl.multiple_of(step * piece, piece))

    def added(offset):
        return joined(wide[pl.ds(offset, piece), :])

    sub_index = lax.broadcasted_iota(jnp.int32, (SUB, 128), 0)
    even = lax.rem(sub_index, 2) == 0

    def apply_grams(picked, gather):
        results = []
        for first in range(0, slots, SUB):
            rows_here = picked[first : first + SUB]
            high = rows_here.astype(BF16).astype(F32)
            stack = jnp.concatenate([high, rows_here - high], axis=0)
            both = jnp.concatenate([even, even], axis=0)
            left = jnp.concatenate(
                [jnp.where(both, stack, 0.0), jnp.where(both, 0.0, stack)], axis=1
            ).astype(BF16)
            result = None
            for pair in range(SUB // 2):
                slot = first + 2 * pair
                product = jnp.dot(
                    left, grams[slot : slot + 2].reshape(256, 256), preferred_element_type=F32
                )
                product = joined(product)
                product = product[:SUB] + product[SUB:]
                result = product if result is None else jnp.where(sub_index // 2 == pair, product, result)
            results.append(result)
        total = jnp.concatenate(results, axis=0)
        gather[orbit] = total
        return total

    one_copy(orbit, partner, 0).wait_recv()
    for step in x_steps:
        one_copy(orbit, partner, xs - 1 + step).wait_recv()
    learned(0, 2)
    for step in both_ways(4):
        signal(known.at[1], column_peer(step))

    edge = 2 * SUB
    tail = tiles - edge
    ahead = jnp.concatenate([hot[0:edge], hot[tail:tiles], match[...].astype(BF16)], axis=0)

    def early(terms):
        return joined(jnp.dot(ahead, halves(terms), preferred_element_type=F32))

    def inverse_of(kappa_part, diagonal_part):
        shifted = kappa_part + 4.0
        return 1.0 / (prior_weight * (shifted * shifted + 4.0) + diagonal_part)

    diagonal = slot_rows(gather_one, slots)
    data = slot_rows(gather_one, 0)
    kap_ahead = jnp.concatenate([kap_own[0:edge], kap_own[tail:tiles], kap_picks[...]], axis=0)
    inverse_ahead = inverse_of(kap_ahead, early(diagonal))
    z_ahead = early(data) * inverse_ahead
    z_edge[...] = z_ahead[: 2 * edge]
    z_halo = [
        halo_copy(z_edge, 2, z_ext, 0, 2, 1, 0, east),
        halo_copy(z_edge, 0, z_ext, rows + 2, 2, 1, 1, west),
    ]
    for copy in z_halo:
        copy.start()
    inverse_picks[...] = inverse_ahead[2 * edge :]
    apply_grams(z_ahead[2 * edge :], gather_two)
    orbit_start(gather_two, 2)

    scatter(diagonal)

    def make_inverse(offset):
        part = pl.ds(offset, piece)
        inverse[part, :] = inverse_of(kap_own[part, :], added(offset))

    each_piece(make_inverse)
    scatter(data)

    def make_z(offset):
        data_part = added(offset)
        right[pl.ds(offset, piece), :] = data_part
        scaled = data_part * inverse[pl.ds(offset, piece), :]
        z_own[pl.ds(offset, piece), :] = scaled
        z_ext[pl.ds(offset + 2 * SUB, piece), :] = scaled

    each_piece(make_z)

    for copy in kap_halo + z_halo:
        copy.wait_recv()

    first_rows = 11

    def first_stencil(ext):
        @pl.loop(0, (rows + 2) // first_rows, unroll=2)
        def _(step):
            row = step * first_rows
            k_ext[pl.ds(pl.multiple_of(row * SUB, SUB), first_rows * SUB), :] = stencil(
                ext, row + 1, kap, row, first_rows
            ).reshape(first_rows * SUB, 128)

    def second_stencil(target):
        @pl.loop(0, rows // SUB, unroll=2)
        def _(step):
            row = step * SUB
            target[pl.ds(pl.multiple_of(row * SUB, SUB), SUB * SUB), :] = prior_weight * stencil(
                k_ext, row + 1, kap, row + 1, SUB
            ).reshape(SUB * SUB, 128)

    first_stencil(z_ext)
    second_stencil(y_own)
    w_ext[0:edge] = jnp.zeros((edge, 128), F32)
    w_ext[tiles + edge : tiles + 2 * edge] = jnp.zeros((edge, 128), F32)
    pick(y_own, picks)

    orbit_wait(gather_two, 2)
    terms = slot_rows(gather_two, 0)
    terms_ahead = early(terms)
    y_ahead = jnp.concatenate([y_own[0:edge], y_own[tail:tiles], picks[...]], axis=0)
    inverse_ahead = jnp.concatenate([inverse[0:edge], inverse[tail:tiles], inverse_picks[...]], axis=0)
    w_ahead = (y_ahead + terms_ahead) * inverse_ahead
    w_edge[...] = w_ahead[: 2 * edge]
    w_halo = [
        halo_copy(w_edge, 2, w_land, 0, 2, 2, 0, east),
        halo_copy(w_edge, 0, w_land, 2, 2, 2, 1, west),
    ]
    for copy in w_halo:
        copy.start()
    w_here = w_ahead[2 * edge :]
    w_terms = apply_grams(w_here, gather_three)
    last = jnp.sum((w_here * w_terms).reshape(slots // SUB, SUB, 128), axis=0)
    scatter(terms)

    def make_w(offset):
        part = pl.ds(offset, piece)
        image = y_own[part, :] + added(offset)
        y_own[part, :] = image
        scaled = image * inverse[part, :]
        w_own[part, :] = scaled
        w_ext[pl.ds(offset + 2 * SUB, piece), :] = scaled

    each_piece(make_w)

    share_rows = rows // orbits
    share_row = orbit * share_rows
    share = pl.ds(pl.multiple_of(share_row * SUB, SUB), share_rows * SUB)

    def folded(product):
        return jnp.sum(product.reshape(share_rows, SUB, 128), axis=0)

    products = [
        folded(right[share, :] * z_own[share, :]),
        folded(y_own[share, :] * z_own[share, :]),
        folded(y_own[share, :] * w_own[share, :]),
    ]
    own_k = stencil(w_ext, share_row + 2, kap, share_row + 1, share_rows)
    head_row, tail_row = w_own[0:SUB], w_own[tiles - SUB : tiles]
    edges = (head_row * head_row + tail_row * tail_row) * (1.0 / orbits)
    products.append(last + prior_weight * (jnp.sum(own_k * own_k, axis=0) + edges))
    lane_index = lax.broadcasted_iota(jnp.int32, (SUB, 128), 1)
    stacked = jnp.zeros((SUB, 128), F32)
    for index, product in enumerate(products):
        stacked = jnp.where(sub_index == index, jnp.sum(product, axis=0, keepdims=True), stacked)

    def folded_lanes(value):
        value = value + pltpu.roll(value, 64, axis=1)
        return value + pltpu.roll(value, 32, axis=1)

    packed = jnp.where(lane_index // 32 == sub_index, folded_lanes(stacked), 0.0)
    plane_stats[me_plane] = jnp.sum(packed, axis=0, keepdims=True)

    def plane_copy(step):
        return pltpu.make_async_remote_copy(
            src_ref=plane_stats.at[me_plane],
            dst_ref=plane_stats.at[me_plane],
            send_sem=plane_send.at[step],
            recv_sem=plane_recv.at[step],
            device_id=plane_peer(step),
            device_id_type=MESH,
        )

    def cross_copy(step):
        return pltpu.make_async_remote_copy(
            src_ref=cross_stats.at[y],
            dst_ref=cross_stats.at[y],
            send_sem=cross_send.at[step],
            recv_sem=cross_recv.at[step],
            device_id=(orbit, lax.rem(y + step, ys) * zs + z),
            device_id_type=MESH,
        )

    def column_copy(step):
        return pltpu.make_async_remote_copy(
            src_ref=column_stats.at[z],
            dst_ref=column_stats.at[z],
            send_sem=column_send.at[step],
            recv_sem=column_recv.at[step],
            device_id=column_peer(step),
            device_id_type=MESH,
        )

    for step in range(1, plane):
        plane_copy(step).start()

    first_k = stencil(w_ext, 2, kap, 1, 1)[0]
    last_k = stencil(w_ext, rows + 1, kap, rows, 1)[0]
    for copy in w_halo:
        copy.wait_recv()
    cross = first_k * w_land[SUB : 2 * SUB] + last_k * w_land[2 * SUB : 3 * SUB]
    cross = folded_lanes(jnp.broadcast_to(jnp.sum(cross, axis=0, keepdims=True), (SUB, 128)))
    cross_stats[y] = jnp.where(lane_row >= 96, (-2.0 * prior_weight) * cross[0:1], 0.0)
    for step in range(1, ys):
        cross_copy(step).start()
    w_ext[0:edge] = w_land[0:edge]
    w_ext[tiles + edge : tiles + 2 * edge] = w_land[edge : 2 * edge]

    orbit_start(gather_three, 3)

    def lay_out(source, target):
        @pl.loop(0, rows // SUB, unroll=2)
        def _(group):
            for tile in range(SUB):
                place = pl.ds(pl.multiple_of(group * SUB, SUB), SUB)
                target[place, tile * 128 : (tile + 1) * 128] = source[
                    pl.ds(group * SUB * SUB + tile, SUB, stride=SUB), :
                ]

    first_stencil(w_ext)
    lay_out(z_own, out_z)
    lay_out(right, out_right)
    lay_out(y_own, out_y)
    lay_out(w_own, out_w)

    @pl.loop(1, plane)
    def _(step):
        plane_copy(step).wait_recv()

    for step in range(1, ys):
        cross_copy(step).wait_recv()
    total = tree_sum([plane_stats[index] for index in range(plane)])
    total = total + tree_sum([cross_stats[index] for index in range(ys)])
    column_stats[z] = total
    learned(1, 4)

    for step in range(1, zs):
        column_copy(step).start()

    second_stencil(q_own)
    orbit_wait(gather_three, 3)
    scatter(slot_rows(gather_three, 0))

    def make_q(offset):
        part = pl.ds(offset, piece)
        q_own[part, :] = q_own[part, :] + added(offset)

    each_piece(make_q)
    lay_out(q_own, out_q)

    for which, buffer in ((0, codes), (2, gather_two), (3, gather_three)):
        for step in range(1, orbits):
            orbit_copy(buffer, which, step).wait_send()
    for copy in own_copies + forwards + kap_halo + z_halo + w_halo:
        copy.wait_send()
    for step in range(1, ys):
        cross_copy(step).wait_send()

    @pl.loop(1, plane)
    def _(step):
        plane_copy(step).wait_send()

    @pl.loop(1, zs)
    def _(step):
        column_copy(step).wait_send()

    @pl.loop(1, zs)
    def _(step):
        column_copy(step).wait_recv()

    total = tree_sum([column_stats[index] for index in range(zs)])
    g = [
        jnp.sum(jnp.where(lane_row // 32 == index, total, 0.0), axis=1, keepdims=True)
        for index in range(4)
    ]
    alpha = g[0] / g[1]
    later = alpha * alpha * g[2] - g[0]
    grow = 1.0 + later / g[0]
    alpha_later = later / (grow * grow * g[1] - 2.0 * grow * alpha * g[2] + alpha * alpha * g[3])
    on_first = alpha + alpha_later * grow
    on_second = alpha_later * alpha

    out_first[...] = on_first
    out_second[...] = on_second


PIECES = 4


def combine(first, second, z, w, right, y, q, out_solution, out_residual, solution_piece, residual_piece, sem):
    rows = z.shape[0] // PIECES
    on_first, on_second = first[...], second[...]
    copies = []
    for piece in range(PIECES):
        part = pl.ds(piece * rows, rows)
        solution_piece[part, :] = on_first * z[part, :] - on_second * w[part, :]
        copies.append(
            pltpu.make_async_copy(solution_piece.at[part], out_solution.at[part], sem.at[0, piece])
        )
        copies[-1].start()
        residual_piece[part, :] = right[part, :] - on_first * y[part, :] + on_second * q[part, :]
        copies.append(
            pltpu.make_async_copy(residual_piece.at[part], out_residual.at[part], sem.at[1, piece])
        )
        copies[-1].start()
    for copy in copies:
        copy.wait()


def solution(mesh):
    return build(mesh, 4, 16)


def build(mesh, ys, zs):
    orbits = mesh.shape["orbit"]

    def per_device(interp, obs_value, obs_weight, block_map, live_count, kappa2):
        slots, _, obs, cells = interp.shape
        rows, lat = kappa2.shape
        tiles = rows * lat // cells
        plane = orbits * ys
        hot_width = max(orbits * slots, 128)
        vmem = pltpu.VMEM
        field = vmem((tiles, 128), F32)
        extended = vmem((tiles + 4 * SUB, 128), F32)
        inner = vmem((tiles + 2 * SUB, 128), F32)
        gather = vmem((orbits, slots, 128), F32)
        z, w, right, y, q, on_first, on_second = pl.pallas_call(
            functools.partial(kernel, (orbits, ys, zs)),
            out_shape=(
                *([pltpu.VMEM(kappa2.shape, F32)] * 5),
                *([pltpu.VMEM((1, 1), F32)] * 2),
            ),
            in_specs=[pl.BlockSpec(memory_space=pltpu.HBM)] * 6,
            out_specs=(pl.BlockSpec(memory_space=vmem),) * 7,
            scratch_shapes=[
                pltpu.SMEM((slots,), jnp.int32),
                pltpu.SMEM((1, 1), jnp.int32),
                vmem((slots, obs, cells), BF16),
                vmem((slots, 1, obs), F32),
                vmem((slots, 1, obs), F32),
                vmem((rows, lat), F32),
                field,
                inner,
                vmem((slots, 128, 256), BF16),
                vmem((tiles, hot_width), BF16),
                vmem((slots, hot_width), F32),
                vmem((orbits, 1, 128), F32),
                vmem((orbits, 2 * slots, 128), F32),
                gather,
                gather,
                field,
                field,
                field,
                vmem((4 * SUB, 128), F32),
                extended,
                inner,
                field,
                field,
                vmem((4 * SUB, 128), F32),
                vmem((4 * SUB, 128), F32),
                extended,
                field,
                vmem((slots, 128), F32),
                vmem((slots, 128), F32),
                vmem((slots, 128), F32),
                vmem((tiles, 256), F32),
                vmem((plane, 1, 128), F32),
                vmem((ys, 1, 128), F32),
                vmem((zs, 1, 128), F32),
                pltpu.SemaphoreType.DMA((5 + CHUNKS,)),
                pltpu.SemaphoreType.DMA((4, orbits)),
                pltpu.SemaphoreType.DMA((4, orbits)),
                pltpu.SemaphoreType.DMA((orbits,)),
                pltpu.SemaphoreType.DMA((orbits,)),
                pltpu.SemaphoreType.DMA((3, 2)),
                pltpu.SemaphoreType.DMA((3, 2)),
                pltpu.SemaphoreType.DMA((plane,)),
                pltpu.SemaphoreType.DMA((plane,)),
                pltpu.SemaphoreType.DMA((ys,)),
                pltpu.SemaphoreType.DMA((ys,)),
                pltpu.SemaphoreType.DMA((zs,)),
                pltpu.SemaphoreType.DMA((zs,)),
                pltpu.SemaphoreType.REGULAR((2,)),
            ],
            compiler_params=pltpu.CompilerParams(
                collective_id=0, has_side_effects=True, vmem_limit_bytes=65600000
            ),
        )(
            interp.reshape(slots, obs, cells),
            obs_value,
            obs_weight,
            block_map.reshape(slots),
            live_count,
            kappa2,
        )
        return pl.pallas_call(
            combine,
            out_shape=(jax.ShapeDtypeStruct(kappa2.shape, F32),) * 2,
            in_specs=[pl.BlockSpec(memory_space=vmem)] * 7,
            out_specs=(pl.BlockSpec(memory_space=pltpu.HBM),) * 2,
            scratch_shapes=[
                vmem(kappa2.shape, F32),
                vmem(kappa2.shape, F32),
                pltpu.SemaphoreType.DMA((2, PIECES)),
            ],
            compiler_params=pltpu.CompilerParams(vmem_limit_bytes=4 * 1024 * 1024),
        )(on_first, on_second, z, w, right, y, q)

    in_specs = (
        P("orbit", "lon", None, None),
        P("orbit", "lon", None),
        P("orbit", "lon", None),
        P("orbit", "lon"),
        P("orbit", "lon"),
        P("lon", None),
    )
    out_specs = (P("lon", None), P("lon", None))
    return jax.shard_map(
        per_device, mesh=mesh, in_specs=in_specs, out_specs=out_specs, check_vma=False
    )
```
